512 devices in a mesh: pipe: 4 (over z_lo), row: 16 (over x, z_hi), col: 8 (over y, core).
Axes of the slice: x: 4, y: 4, z: 16 (z_hi: 4, z_lo: 4; z = z_hi * 4 + z_lo), core: 2. Of those that a mesh axis runs over, the one named last changes fastest.
Arguments:
- saved_in: bfloat16 [4, 128, 128, 2048], P('pipe', 'row', 'col'), may hold values from -400 to 400
- cotangent: bfloat16 [4, 128, 128, 2048], P('pipe', 'row', 'col'), may hold values from -6 to 6
- section_gains: float32 [4, 5, 2048], P('pipe'), may hold values from -8 to 8
Outputs:
- next_grad: bfloat16 [4, 128, 128, 2048], P('pipe', 'row', 'col')
The draws below stay inside these ranges and needn't reach their ends.
All inputs are finite; a program needn't handle non-finite values.
Results may differ from the reference program's by a relative error of at most 0.0028.
The reference program's roundings to bfloat16 on the way count: a program that leaves them out, or rounds other values in their place, can miss the bound.
Values may be sent and summed in bfloat16 or wider, within the bound.
A program may use at most 64 MiB of HBM per device.

```python
import math
import jax
import jax.numpy as jnp
from jax import lax

D = 2048
HEADS = 16
HEAD_DIM = 128
TILE = 8
SPAN = 5
IMG_ROWS = 128
IMG_COLS = 128
N_PIPE = 4


def draw_image(key, salt):
    keys = jax.random.split(jax.random.fold_in(key, salt), 3)
    shape = (N_PIPE, IMG_ROWS, IMG_COLS, D)
    base = jnp.clip(jax.random.normal(keys[0], shape, jnp.float32), -4.0, 4.0)
    row_scale = jnp.exp(jax.random.uniform(keys[1], (N_PIPE, IMG_ROWS, IMG_COLS, 1), jnp.float32, math.log(0.3), math.log(3.0)))
    col_scale = jnp.exp(jax.random.uniform(keys[2], (N_PIPE, 1, 1, D), jnp.float32, math.log(0.3), math.log(3.0)))
    return (base * row_scale * col_scale).astype(jnp.bfloat16)


def draw_saved_in(key, part):
    return draw_image(key, 23)


def draw_section_gains(key, part):
    keys = jax.random.split(jax.random.fold_in(key, 37), 9)
    shape = (N_PIPE, 1, D)
    norm_gain = jnp.exp(jax.random.uniform(keys[0], shape, jnp.float32, math.log(0.5), math.log(2.0)))
    query_gain = jnp.clip(jax.random.normal(keys[3], shape, jnp.float32), -3.0, 3.0)
    key_gain = jnp.clip(jax.random.normal(keys[5], shape, jnp.float32), -3.0, 3.0)
    value_gain = jnp.clip(jax.random.normal(keys[7], shape, jnp.float32), -3.0, 3.0)
    output_gain = jnp.clip(jax.random.normal(keys[8], shape, jnp.float32), -3.0, 3.0)
    stacked = jnp.concatenate([norm_gain, query_gain, key_gain, value_gain, output_gain], axis=1)
    return jnp.clip(stacked, -8.0, 8.0).astype(jnp.float32)


def block_scale(own_key, shape, shards, low, top_value):
    def one(dim, blocks):
        steps = jax.random.uniform(jax.random.fold_in(jax.random.fold_in(own_key, 6), dim), (blocks,), jnp.float32, low / len(shards), top_value / len(shards))
        return jnp.repeat(jnp.exp(steps), shape[dim] // blocks).reshape((-1,) + (1,) * (len(shape) - dim - 1))

    level = one(*shards[0])
    for cut in shards[1:]:
        level = level * one(*cut)
    return level


def noise(stream_key, dims, scale, limit, cuts=(), kind=jnp.bfloat16):
    drawn = scale * jax.random.normal(stream_key, dims, jnp.float32)
    if cuts:
        drawn = drawn * block_scale(stream_key, dims, cuts, -0.22, 0.18)
    return jnp.clip(drawn, -limit, limit).astype(kind)


def setup_inputs(seed: int = 0) -> dict:
    seeds = jax.random.split(jax.random.key(seed), 4)
    return {
        "saved_in": draw_saved_in(jax.random.fold_in(seeds[3], 71), 0),
        "cotangent": noise(seeds[1], (N_PIPE, IMG_ROWS, IMG_COLS, D), 1.0, 6.0, ((0, 4), (1, 16), (2, 8))),
        "section_gains": draw_section_gains(jax.random.fold_in(seeds[3], 71), 0),
    }


NEGATIVE = -1e+30
EPSILON = 1e-06

def to_tiles(image):
    height, width, channels = image.shape
    image = image.reshape(height // TILE, TILE, width // TILE, TILE, channels)
    return image.transpose(0, 2, 1, 3, 4).reshape(height // TILE, width // TILE, TILE * TILE, channels)

def from_tiles(tiled):
    tile_rows, tile_cols, area, channels = tiled.shape
    tiled = tiled.reshape(tile_rows, tile_cols, TILE, TILE, channels)
    return tiled.transpose(0, 2, 1, 3, 4).reshape(tile_rows * TILE, tile_cols * TILE, channels)

def windows(extended, tile_rows, tile_cols):
    return jnp.concatenate([extended[row_off:row_off + tile_rows, col_off:col_off + tile_cols] for row_off in range(SPAN) for col_off in range(SPAN)], axis=2)

def key_valid(base_row, base_col, tile_rows, tile_cols, all_rows, all_cols):
    reach_tiles = SPAN // 2
    offsets = jnp.arange(SPAN, dtype=jnp.int32) - reach_tiles
    row_ids = base_row + jnp.arange(tile_rows, dtype=jnp.int32)[:, None] + offsets[None, :]
    col_ids = base_col + jnp.arange(tile_cols, dtype=jnp.int32)[:, None] + offsets[None, :]
    row_ok = (row_ids >= 0) & (row_ids < all_rows)
    col_ok = (col_ids >= 0) & (col_ids < all_cols)
    allowed = row_ok[:, None, :, None] & col_ok[None, :, None, :]
    return jnp.repeat(allowed.reshape(tile_rows, tile_cols, SPAN * SPAN), TILE * TILE, axis=2)

def split_heads(array):
    return array.reshape(array.shape[:-1] + (HEADS, array.shape[-1] // HEADS))

def contract(form, left, right):
    return jnp.einsum(form, left.astype(jnp.float32), right.astype(jnp.float32), precision=lax.Precision.HIGHEST)

def project(normed, scales, factor):
    return (normed.astype(jnp.float32) * (scales * factor)).astype(jnp.bfloat16)

def normalize(image, scales):
    x_float = image.astype(jnp.float32)
    inverse = lax.rsqrt(lax.optimization_barrier(jnp.mean(x_float * x_float, axis=-1, keepdims=True)) + EPSILON)
    return (x_float, inverse, (x_float * inverse * scales).astype(jnp.bfloat16))

def attend(queries, key_win, value_win, allowed):
    scores = contract('ijqhc,ijkhc->ijhqk', split_heads(queries), split_heads(key_win))
    scores = jnp.where(allowed[:, :, None, None, :], scores, NEGATIVE)
    row_max = lax.optimization_barrier(jnp.max(scores, axis=-1, keepdims=True))
    log_total = row_max + jnp.log(lax.optimization_barrier(jnp.sum(jnp.exp(scores - row_max), axis=-1, keepdims=True)))
    weights = jnp.exp(scores - log_total)
    rounded = weights.astype(jnp.bfloat16)
    output = contract('ijhqk,ijkhc->ijqhc', rounded, split_heads(value_win))
    return (log_total, weights, rounded, output.reshape(queries.shape))

def prepare(image, scales):
    tiled = to_tiles(image)
    reach_tiles = SPAN // 2
    factor = 1.0 / math.sqrt(HEAD_DIM)
    x_float, inverse, normed = normalize(tiled, scales[0])
    padded = jnp.pad(normed, ((reach_tiles, reach_tiles), (reach_tiles, reach_tiles), (0, 0), (0, 0)))
    queries = project(normed, scales[1], factor)
    keys_ext = project(padded, scales[2], 1.0)
    values_ext = project(padded, scales[3], 1.0)
    return (tiled, x_float, inverse, padded, queries, keys_ext, values_ext)

def row_attention(queries, keys_ext, values_ext, index, tile_rows, tile_cols):
    allowed = key_valid(index, 0, 1, tile_cols, tile_rows, tile_cols)
    key_win = windows(lax.dynamic_slice_in_dim(keys_ext, index, SPAN, 0), 1, tile_cols)
    value_win = windows(lax.dynamic_slice_in_dim(values_ext, index, SPAN, 0), 1, tile_cols)
    query_row = lax.dynamic_slice_in_dim(queries, index, 1, 0)
    return (query_row, key_win, value_win, attend(query_row, key_win, value_win, allowed))

def backward_image(image, upstream_image, scales):
    tiled, x_float, inverse, padded, queries, keys_ext, values_ext = prepare(image, scales)
    tile_rows, tile_cols = (tiled.shape[0], tiled.shape[1])
    factor = 1.0 / math.sqrt(HEAD_DIM)
    tile_area = TILE * TILE
    upstream = to_tiles(upstream_image).astype(jnp.float32)
    out_grad = (upstream * scales[4]).astype(jnp.bfloat16)

    def one_row(spread, index):
        query_row, key_win, value_win, parts = row_attention(queries, keys_ext, values_ext, index, tile_rows, tile_cols)
        log_total, weights, rounded, output = parts
        grad_row = lax.dynamic_slice_in_dim(out_grad, index, 1, 0)
        delta_sum = lax.optimization_barrier(jnp.sum(split_heads(grad_row.astype(jnp.float32)) * split_heads(output), axis=-1))
        prob_grad = contract('ijqhc,ijkhc->ijhqk', split_heads(grad_row), split_heads(value_win))
        dscore = (weights * (prob_grad - jnp.swapaxes(delta_sum, 2, 3)[..., None])).astype(jnp.bfloat16)
        dquery = contract('ijhqk,ijkhc->ijqhc', dscore, split_heads(key_win)).reshape(query_row.shape)
        key_grad = contract('ijhqk,ijqhc->ijkhc', dscore, split_heads(query_row)).reshape(key_win.shape)
        dvalue = contract('ijhqk,ijqhc->ijkhc', rounded, split_heads(grad_row)).reshape(key_win.shape)
        terms = key_grad * scales[2] + dvalue * scales[3]
        slab = lax.dynamic_slice_in_dim(spread, index, SPAN, 0)
        for row_off in range(SPAN):
            for col_off in range(SPAN):
                offset_id = row_off * SPAN + col_off
                slab = slab.at[row_off:row_off + 1, col_off:col_off + tile_cols].add(terms[:, :, offset_id * tile_area:(offset_id + 1) * tile_area])
        spread = lax.dynamic_update_slice_in_dim(spread, slab, index, 0)
        return (spread, (dquery * (scales[1] * factor))[0])
    spread, dquery_all = lax.scan(one_row, jnp.zeros(padded.shape, jnp.float32), jnp.arange(tile_rows, dtype=jnp.int32))
    reach_tiles = SPAN // 2
    dnormed = dquery_all + spread[reach_tiles:reach_tiles + tile_rows, reach_tiles:reach_tiles + tile_cols]
    scaled = scales[0] * dnormed
    image_grad = upstream + inverse * scaled - x_float * (inverse * inverse * inverse) * lax.optimization_barrier(jnp.mean(x_float * scaled, axis=-1, keepdims=True))
    return from_tiles(image_grad.astype(jnp.bfloat16))

def reference(saved_in, cotangent, section_gains):
    gradients = [backward_image(saved_in[segment], cotangent[segment], section_gains[segment]) for segment in range(N_PIPE)]
    zeros_image = jnp.zeros_like(gradients[0])
    return jnp.stack(gradients[1:] + [zeros_image])
```

```python
import functools
import math

import jax
import jax.numpy as jnp
from jax import lax
from jax.experimental import pallas as pl
from jax.experimental.pallas import tpu as pltpu
from jax.sharding import PartitionSpec as P

HEADS = 16
HEAD_DIM = 128
TILE = 8
SPAN = 5
REACH = SPAN // 2

NEGATIVE = -1e30
EPSILON = 1e-06
F32 = jnp.float32
BF16 = jnp.bfloat16


def dot(left, right, dims):
    return lax.dot_general(left, right, (dims, ((), ())), preferred_element_type=F32)


def fold(block, op):
    rows, lanes = block.shape
    return op(block.reshape(rows // 8, 8, lanes), axis=0)


def attention_kernel(
    x3_ref, r3_ref, cot_ref, gains_ref, own_ref, left_ref, right_ref,
    kv_ref, kt_ref, qd_ref, w_ref, st_ref, bias_ref,
):
    rows, area, depth = cot_ref.shape
    wide = 3 * area
    col = lax.axis_index("col")
    cols = lax.axis_size("col")
    gn = gains_ref[0:1, :]
    gq = gains_ref[1:2, :]
    gk = gains_ref[2:3, :]
    gv = gains_ref[3:4, :]
    go = gains_ref[4:5, :]

    key = lax.broadcasted_iota(jnp.int32, (wide, area), 0)
    query = lax.broadcasted_iota(jnp.int32, (wide, area), 1)
    key_tile = 2 * (key // area) + (key // TILE) % 2
    query_tile = (query // TILE) % 2
    near = (key_tile >= query_tile) & (key_tile <= query_tile + 2 * REACH)
    inside = (col * 2 + key_tile >= REACH) & (col * 2 + key_tile < 2 * cols + REACH)
    bias_ref[0] = jnp.full((wide, area), NEGATIVE, F32)
    bias_ref[1] = jnp.where(near & inside, 0.0, NEGATIVE)

    for pad in (0, 1, rows + 2, rows + 3):
        kv_ref[pad] = jnp.zeros((wide, 2 * depth), BF16)
        kt_ref[pad] = jnp.zeros((depth, wide), BF16)
        qd_ref[pad] = jnp.zeros((2 * area, 2 * depth), BF16)
    for key_row, slot in ((0, 0), (0, 1), (1, 0), (rows - 2, 4), (rows - 1, 3), (rows - 1, 4)):
        w_ref[key_row + REACH, :, slot * 2 * area : (slot + 1) * 2 * area] = jnp.zeros(
            (wide, 2 * area), BF16
        )

    def prepare(row, carry):
        for block in range(3):
            inverse = jnp.broadcast_to(r3_ref[block, pl.ds(row, 1), :], (area, area)).T
            x_float = x3_ref[block, row].astype(F32)
            normed = (x_float * inverse * gn).astype(BF16).astype(F32)
            keys = (normed * gk).astype(BF16)
            lanes = slice(block * area, (block + 1) * area)
            kv_ref[row + REACH, lanes, :depth] = keys
            kv_ref[row + REACH, lanes, depth:] = (normed * gv).astype(BF16)
            kt_ref[row + REACH, :, lanes] = keys.T
            if block == 1:
                qd_ref[row + REACH, :area, :depth] = (normed * gq).astype(BF16)
                qd_ref[row + REACH, :area, depth:] = jnp.zeros((area, depth), BF16)
                qd_ref[row + REACH, area:, :depth] = jnp.zeros((area, depth), BF16)
                qd_ref[row + REACH, area:, depth:] = (cot_ref[row].astype(F32) * go).astype(BF16)
        return carry

    lax.fori_loop(0, rows, prepare, 0)

    def query_row(row, carry):
        qd = qd_ref[row + REACH]
        top = jnp.full((8, area), NEGATIVE, F32)
        for off in range(SPAN):
            far = row + off - REACH
            valid = jnp.logical_and(far >= 0, far < rows).astype(jnp.int32)
            pair = dot(kv_ref[row + off], qd, ((1,), (1,)))
            scores = pair[:, :area] + bias_ref[valid]
            st_ref[off, :, :area] = scores
            st_ref[off, :, area:] = pair[:, area:]
            top = jnp.maximum(top, fold(scores, jnp.max))
        top = jnp.max(top, axis=0, keepdims=True)
        total = jnp.zeros((8, area), F32)
        for off in range(SPAN):
            raised = jnp.exp(st_ref[off, :, :area] - top)
            st_ref[off, :, :area] = raised
            total = total + fold(raised, jnp.sum)
        scale = 1.0 / jnp.sum(total, axis=0, keepdims=True)
        delta = jnp.zeros((8, area), F32)
        for off in range(SPAN):
            rounded = (st_ref[off, :, :area] * scale).astype(BF16)
            slot = SPAN - 1 - off
            w_ref[row + off, :, slot * 2 * area + area : (slot + 1) * 2 * area] = rounded
            delta = delta + fold(rounded.astype(F32) * st_ref[off, :, area:], jnp.sum)
        delta = jnp.sum(delta, axis=0, keepdims=True)
        turned = jnp.zeros((depth, area), F32)
        for off in range(SPAN):
            weights = st_ref[off, :, :area] * scale
            dscore = (weights * (st_ref[off, :, area:] - delta)).astype(BF16)
            slot = SPAN - 1 - off
            w_ref[row + off, :, slot * 2 * area : slot * 2 * area + area] = dscore
            turned = turned + dot(kt_ref[row + off], dscore, ((1,), (0,)))
        own_ref[row] = turned.T * gq
        return carry

    lax.fori_loop(0, rows, query_row, 0)

    def key_row(row, carry):
        queries = qd_ref[pl.ds(row, SPAN)].reshape(SPAN * 2 * area, 2 * depth)
        grads = dot(w_ref[row + REACH], queries, ((1,), (0,)))
        terms = grads[:, :depth] * gk + grads[:, depth:] * gv
        left_ref[row] = terms[:area]
        own_ref[row] = own_ref[row] + terms[area : 2 * area]
        right_ref[row] = terms[2 * area :]
        return carry

    lax.fori_loop(0, rows, key_row, 0)


def attention(x3, r3, cot, gains):
    rows, area, depth = cot.shape
    wide = 3 * area
    block = jax.ShapeDtypeStruct((rows, area, depth), F32)
    vmem = pl.BlockSpec(memory_space=pltpu.VMEM)
    return pl.pallas_call(
        attention_kernel,
        out_shape=(block, block, block),
        in_specs=[vmem] * 4,
        out_specs=(vmem, vmem, vmem),
        scratch_shapes=[
            pltpu.VMEM((rows + 4, wide, 2 * depth), BF16),
            pltpu.VMEM((rows + 4, depth, wide), BF16),
            pltpu.VMEM((rows + 4, 2 * area, 2 * depth), BF16),
            pltpu.VMEM((rows + 4, wide, SPAN * 2 * area), BF16),
            pltpu.VMEM((SPAN, wide, 2 * area), F32),
            pltpu.VMEM((2, wide, area), F32),
        ],
        compiler_params=pltpu.CompilerParams(vmem_limit_bytes=60 * 1024 * 1024),
        name="head_attention",
    )(x3, r3, cot, gains)


def shift(block, axis, distance):
    size = lax.axis_size(axis)
    route = [(i, i + distance) for i in range(size) if 0 <= i + distance < size]
    return lax.ppermute(block, axis, route)


def per_device(saved_in, cotangent, section_gains):
    _, tall, across, width = saved_in.shape
    area = tall * across
    factor = 1.0 / math.sqrt(HEAD_DIM)
    head = lax.axis_index("row")
    x = saved_in.reshape(area, width)
    cot = cotangent.reshape(area, width)
    x_float = x.astype(F32)
    inverse = lax.rsqrt(jnp.mean(x_float * x_float, axis=-1) + EPSILON)

    def by_head(block):
        return block.reshape(area, HEADS, HEAD_DIM).transpose(1, 0, 2)

    packed = jnp.stack([by_head(x), by_head(cot)], axis=1)
    packed = lax.all_to_all(packed, "row", 0, 0)
    inverse = lax.all_gather(inverse, "row")
    x_head = packed[:, 0]
    cot_head = packed[:, 1]
    x3 = jnp.stack([shift(x_head, "col", 1), x_head, shift(x_head, "col", -1)])
    r3 = jnp.stack([shift(inverse, "col", 1), inverse, shift(inverse, "col", -1)])
    gains = lax.dynamic_slice_in_dim(section_gains[0], head * HEAD_DIM, HEAD_DIM, 1)
    gains = gains * jnp.array([1.0, factor, 1.0, 1.0, 1.0], F32)[:, None]
    gains = jnp.concatenate([gains, jnp.zeros((3, HEAD_DIM), F32)], axis=0)
    own, left, right = attention(x3, r3, cot_head, gains)
    dnormed = own + shift(left, "col", -1) + shift(right, "col", 1)
    scaled = dnormed * gains[0]
    x_head = x_head.astype(F32)
    mean = lax.psum(jnp.sum(x_head * scaled, axis=-1), "row") / width
    inv = inverse[..., None]
    grad = cot_head.astype(F32) + inv * scaled - x_head * (inv * inv * inv) * mean[..., None]
    grad = lax.all_to_all(grad.astype(BF16), "row", 0, 0)
    grad = grad.transpose(1, 0, 2).reshape(1, tall, across, width)
    return shift(grad, "pipe", -1)


def solution(mesh):
    return jax.shard_map(
        per_device,
        mesh=mesh,
        in_specs=(
            P("pipe", "row", "col", None),
            P("pipe", "row", "col", None),
            P("pipe", None, None),
        ),
        out_specs=P("pipe", "row", "col", None),
        check_vma=False,
    )
```

```python
import math

import jax
import jax.numpy as jnp
from jax import lax
from jax.experimental import pallas as pl
from jax.experimental.pallas import tpu as pltpu
from jax.sharding import PartitionSpec as P

HEADS = 16
HEAD_DIM = 128
TILE = 8
SPAN = 5
REACH = SPAN // 2

NEGATIVE = -1e30
EPSILON = 1e-06
F32 = jnp.float32
BF16 = jnp.bfloat16
MESH = pl.DeviceIdType.MESH


def dot(left, right, dims):
    return lax.dot_general(left, right, (dims, ((), ())), preferred_element_type=F32)


def fold(block, op):
    rows, lanes = block.shape
    return op(block.reshape(rows // 8, 8, lanes), axis=0)


def head_gains(gains_ref):
    start = pl.multiple_of(lax.axis_index("row") * HEAD_DIM, HEAD_DIM)
    return gains_ref[:, pl.ds(start, HEAD_DIM)]


def attention_kernel(*refs):
    @pl.when(lax.axis_index("pipe") > 0)
    def _():
        attention_body(*refs)


def attention_body(
    x3_ref, r3_ref, cot_ref, gains_ref, own_ref, left_ref, right_ref,
    kv_ref, kt_ref, qd_ref, w_ref, st_ref, bias_ref,
):
    rows, area, depth = cot_ref.shape
    wide = 3 * area
    col = lax.axis_index("col")
    cols = lax.axis_size("col")
    gains = head_gains(gains_ref)
    gn = gains[0:1, :]
    gq = gains[1:2, :] * (1.0 / math.sqrt(HEAD_DIM))
    gk = gains[2:3, :]
    gv = gains[3:4, :]
    go = gains[4:5, :]

    key = lax.broadcasted_iota(jnp.int32, (wide, area), 0)
    query = lax.broadcasted_iota(jnp.int32, (wide, area), 1)
    key_tile = 2 * (key // area) + (key // TILE) % 2
    query_tile = (query // TILE) % 2
    near = (key_tile >= query_tile) & (key_tile <= query_tile + 2 * REACH)
    inside = (col * 2 + key_tile >= REACH) & (col * 2 + key_tile < 2 * cols + REACH)
    bias_ref[0] = jnp.full((wide, area), NEGATIVE, F32)
    bias_ref[1] = jnp.where(near & inside, 0.0, NEGATIVE)

    for pad in (0, 1, rows + 2, rows + 3):
        kv_ref[pad] = jnp.zeros((wide, 2 * depth), BF16)
        kt_ref[pad] = jnp.zeros((depth, wide), BF16)
        qd_ref[pad] = jnp.zeros((2 * area, 2 * depth), BF16)
    for key_row, slot in ((0, 0), (0, 1), (1, 0), (rows - 2, 4), (rows - 1, 3), (rows - 1, 4)):
        w_ref[key_row + REACH, :, slot * 2 * area : (slot + 1) * 2 * area] = jnp.zeros(
            (wide, 2 * area), BF16
        )

    def prepare(row, carry):
        for block in range(3):
            inverse = jnp.broadcast_to(r3_ref[block, row, 0:1, :], (area, area)).T
            x_float = x3_ref[block, row].astype(F32)
            normed = (x_float * inverse * gn).astype(BF16).astype(F32)
            if block != 1:
                present = col > 0 if block == 0 else col < cols - 1
                normed = jnp.where(present, normed, 0.0)
            keys = (normed * gk).astype(BF16)
            lanes = slice(block * area, (block + 1) * area)
            kv_ref[row + REACH, lanes, :depth] = keys
            kv_ref[row + REACH, lanes, depth:] = (normed * gv).astype(BF16)
            kt_ref[row + REACH, :, lanes] = keys.T
            if block == 1:
                qd_ref[row + REACH, :area, :depth] = (normed * gq).astype(BF16)
                qd_ref[row + REACH, :area, depth:] = jnp.zeros((area, depth), BF16)
                qd_ref[row + REACH, area:, :depth] = jnp.zeros((area, depth), BF16)
                qd_ref[row + REACH, area:, depth:] = (cot_ref[row].astype(F32) * go).astype(BF16)
        return carry

    lax.fori_loop(0, rows, prepare, 0)

    def query_row(row, carry):
        qd = qd_ref[row + REACH]
        top = jnp.full((8, area), NEGATIVE, F32)
        for off in range(SPAN):
            far = row + off - REACH
            valid = jnp.logical_and(far >= 0, far < rows).astype(jnp.int32)
            pair = dot(kv_ref[row + off], qd, ((1,), (1,)))
            scores = pair[:, :area] + bias_ref[valid]
            st_ref[off, :, :area] = scores
            st_ref[off, :, area:] = pair[:, area:]
            top = jnp.maximum(top, fold(scores, jnp.max))
        top = jnp.max(top, axis=0, keepdims=True)
        total = jnp.zeros((8, area), F32)
        for off in range(SPAN):
            raised = jnp.exp(st_ref[off, :, :area] - top)
            st_ref[off, :, :area] = raised
            total = total + fold(raised, jnp.sum)
        scale = 1.0 / jnp.sum(total, axis=0, keepdims=True)
        delta = jnp.zeros((8, area), F32)
        for off in range(SPAN):
            rounded = (st_ref[off, :, :area] * scale).astype(BF16)
            slot = SPAN - 1 - off
            w_ref[row + off, :, slot * 2 * area + area : (slot + 1) * 2 * area] = rounded
            delta = delta + fold(rounded.astype(F32) * st_ref[off, :, area:], jnp.sum)
        delta = jnp.sum(delta, axis=0, keepdims=True)
        turned = jnp.zeros((depth, area), F32)
        for off in range(SPAN):
            weights = st_ref[off, :, :area] * scale
            dscore = (weights * (st_ref[off, :, area:] - delta)).astype(BF16)
            slot = SPAN - 1 - off
            w_ref[row + off, :, slot * 2 * area : slot * 2 * area + area] = dscore
            turned = turned + dot(kt_ref[row + off], dscore, ((1,), (0,)))
        own_ref[row] = turned.T * gq
        return carry

    lax.fori_loop(0, rows, query_row, 0)

    def key_row(row, carry):
        queries = qd_ref[pl.ds(row, SPAN)].reshape(SPAN * 2 * area, 2 * depth)
        grads = dot(w_ref[row + REACH], queries, ((1,), (0,)))
        terms = grads[:, :depth] * gk + grads[:, depth:] * gv
        left_ref[row] = terms[:area]
        own_ref[row] = own_ref[row] + terms[area : 2 * area]
        right_ref[row] = terms[2 * area :]
        return carry

    lax.fori_loop(0, rows, key_row, 0)


def attention(x3, r3, cot, gains):
    rows, area, depth = cot.shape
    wide = 3 * area
    block = jax.ShapeDtypeStruct((rows, area, depth), F32)
    vmem = pl.BlockSpec(memory_space=pltpu.VMEM)
    return pl.pallas_call(
        attention_kernel,
        out_shape=(block, block, block),
        in_specs=[vmem] * 4,
        out_specs=(vmem, vmem, vmem),
        scratch_shapes=[
            pltpu.VMEM((rows + 4, wide, 2 * depth), BF16),
            pltpu.VMEM((rows + 4, depth, wide), BF16),
            pltpu.VMEM((rows + 4, 2 * area, 2 * depth), BF16),
            pltpu.VMEM((rows + 4, wide, SPAN * 2 * area), BF16),
            pltpu.VMEM((SPAN, wide, 2 * area), F32),
            pltpu.VMEM((2, wide, area), F32),
        ],
        compiler_params=pltpu.CompilerParams(vmem_limit_bytes=60 * 1024 * 1024),
        name="head_attention",
    )(x3, r3, cot, gains)


def greet(devices):
    barrier = pltpu.get_barrier_semaphore()
    for device in devices:
        pl.semaphore_signal(barrier, inc=1, device_id=device, device_id_type=MESH)


def greet_rows(others):
    barrier = pltpu.get_barrier_semaphore()
    me = lax.axis_index("row")

    def step(hop, carry):
        pl.semaphore_signal(
            barrier, inc=1, device_id={"row": lax.rem(me + hop, HEADS)}, device_id_type=MESH
        )
        return carry

    lax.fori_loop(1, others + 1, step, 0)


def head_lanes(head):
    return pl.ds(pl.multiple_of(head * HEAD_DIM, HEAD_DIM), HEAD_DIM)


def remote(src, dst, send, recv, device):
    return pltpu.make_async_remote_copy(
        src_ref=src, dst_ref=dst, send_sem=send, recv_sem=recv,
        device_id=device, device_id_type=MESH,
    )


def gather_kernel(*refs):
    @pl.when(lax.axis_index("pipe") > 0)
    def _():
        gather_body(*refs)


def gather_body(
    x_ref, x_far, cot_far, x3_ref, r3_ref, cot_ref, inv_ref,
    local_sem, x_send, x_recv, r_send, r_recv, c_send, c_recv,
    fx_send, fx_recv, fr_send, fr_recv,
):
    me = lax.axis_index("row")
    col = lax.axis_index("col")
    cols = lax.axis_size("col")
    area = x_ref.shape[0]
    barrier = pltpu.get_barrier_semaphore()
    greet_rows(HEADS - 1)

    @pl.when(col > 0)
    def _():
        greet([{"col": col - 1}])

    @pl.when(col < cols - 1)
    def _():
        greet([{"col": col + 1}])

    own_x = pltpu.make_async_copy(x_far.at[:, head_lanes(me)], x3_ref.at[1, me], local_sem.at[0])
    own_c = pltpu.make_async_copy(cot_far.at[:, head_lanes(me)], cot_ref.at[me], local_sem.at[1])
    own_x.start()
    own_c.start()
    x_float = x_ref[...].astype(F32)
    square = jnp.mean(x_float * x_float, axis=-1, keepdims=True)
    inverse = jnp.broadcast_to(lax.rsqrt(square + EPSILON), (area, area))
    inv_ref[...] = inverse.T[:8]
    own_r = pltpu.make_async_copy(inv_ref, r3_ref.at[1, me], local_sem.at[2])
    pl.semaphore_wait(
        barrier, HEADS - 1 + (col > 0).astype(jnp.int32) + (col < cols - 1).astype(jnp.int32)
    )

    def x_copy(src, dst):
        return remote(
            x_far.at[:, head_lanes(dst)], x3_ref.at[1, src], x_send.at[dst], x_recv.at[src],
            {"row": dst},
        )

    def r_copy(src, dst):
        return remote(inv_ref, r3_ref.at[1, src], r_send.at[dst], r_recv.at[src], {"row": dst})

    def c_copy(src, dst):
        return remote(
            cot_far.at[:, head_lanes(dst)], cot_ref.at[src], c_send.at[dst], c_recv.at[src],
            {"row": dst},
        )

    def to(hop):
        return lax.rem(me + hop, HEADS)

    def back(hop):
        return lax.rem(me + HEADS - hop, HEADS)

    def start_x(hop, carry):
        x_copy(me, to(hop)).start()
        return carry

    def start_rest(hop, carry):
        c_copy(me, to(hop)).start()
        return carry

    def start_r(hop, carry):
        r_copy(me, to(hop)).start()
        return carry

    lax.fori_loop(1, HEADS, start_x, 0)
    lax.fori_loop(1, HEADS, start_r, 0)
    own_r.start()
    lax.fori_loop(1, HEADS, start_rest, 0)

    def beside(src, side):
        device = {"col": col - 1} if side == 0 else {"col": col + 1}
        slot = 2 - 2 * side
        return (
            remote(
                x3_ref.at[1, src], x3_ref.at[slot, src], fx_send.at[side, src],
                fx_recv.at[side, src], device,
            ),
            remote(
                r3_ref.at[1, src], r3_ref.at[slot, src], fr_send.at[side, src],
                fr_recv.at[side, src], device,
            ),
        )

    def forward(src):
        @pl.when(col > 0)
        def _():
            for copy in beside(src, 0):
                copy.start()

        @pl.when(col < cols - 1)
        def _():
            for copy in beside(src, 1):
                copy.start()

    own_x.wait()
    own_r.wait()
    forward(me)

    def pass_on(hop, carry):
        src = back(hop)
        x_copy(src, me).wait_recv()
        r_copy(src, me).wait_recv()
        forward(src)
        return carry

    lax.fori_loop(1, HEADS, pass_on, 0)

    def finish(hop, carry):
        x_copy(me, to(hop)).wait_send()
        r_copy(me, to(hop)).wait_send()
        c_copy(me, to(hop)).wait_send()
        c_copy(back(hop), me).wait_recv()
        return carry

    lax.fori_loop(1, HEADS, finish, 0)
    own_c.wait()

    def finish_beside(src, carry):
        @pl.when(col > 0)
        def _():
            for copy in beside(src, 0):
                copy.wait_send()
            for copy in beside(src, 1):
                copy.wait_recv()

        @pl.when(col < cols - 1)
        def _():
            for copy in beside(src, 1):
                copy.wait_send()
            for copy in beside(src, 0):
                copy.wait_recv()

        return carry

    lax.fori_loop(0, HEADS, finish_beside, 0)


def gather(x, cot):
    area = x.shape[0]
    far = pl.BlockSpec(memory_space=pl.ANY)
    vmem = pl.BlockSpec(memory_space=pltpu.VMEM)
    dma = pltpu.SemaphoreType.DMA
    return pl.pallas_call(
        gather_kernel,
        out_shape=(
            jax.ShapeDtypeStruct((3, HEADS, area, HEAD_DIM), BF16),
            jax.ShapeDtypeStruct((3, HEADS, 8, area), F32),
            jax.ShapeDtypeStruct((HEADS, area, HEAD_DIM), BF16),
        ),
        in_specs=[vmem, far, far],
        out_specs=(far, far, far),
        scratch_shapes=[
            pltpu.VMEM((8, area), F32),
            dma((3,)),
            dma((HEADS,)), dma((HEADS,)), dma((HEADS,)), dma((HEADS,)), dma((HEADS,)), dma((HEADS,)),
            dma((2, HEADS)), dma((2, HEADS)), dma((2, HEADS)), dma((2, HEADS)),
        ],
        compiler_params=pltpu.CompilerParams(collective_id=0, has_side_effects=True),
        name="gather_heads",
    )(x, x, cot)


PARTS = 4


def scatter_kernel(
    own_ref, left_far, right_far, x3_far, r3_far, cot_ref, gains_ref, out_ref,
    x_ref, r_ref, from_ref, scaled_ref, mean_ref, means_ref, grad_ref,
    local_sem, t_send, t_recv, m_send, m_recv, g_send, g_recv,
):
    me = lax.axis_index("row")
    col = lax.axis_index("col")
    cols = lax.axis_size("col")
    pipe = lax.axis_index("pipe")
    pipes = lax.axis_size("pipe")
    rows, area, depth = own_ref.shape
    width = rows * depth
    span = rows // PARTS
    barrier = pltpu.get_barrier_semaphore()

    def grad_copy(src, dst):
        return remote(
            grad_ref.at[dst], out_ref.at[:, head_lanes(src)], g_send.at[dst], g_recv.at[src],
            {"pipe": pipe - 1, "row": dst},
        )

    @pl.when(pipe < pipes - 1)
    def _():
        def step(row, carry):
            pl.semaphore_signal(
                barrier, inc=1, device_id={"pipe": pipe + 1, "row": row}, device_id_type=MESH
            )
            return carry

        lax.fori_loop(0, rows, step, 0)

    @pl.when(pipe > 0)
    def _():
        greet_rows(HEADS - 1)

        @pl.when(col > 0)
        def _():
            greet([{"col": col - 1}])

        @pl.when(col < cols - 1)
        def _():
            greet([{"col": col + 1}])

        load_x = pltpu.make_async_copy(x3_far.at[1], x_ref, local_sem.at[0])
        load_r = pltpu.make_async_copy(r3_far.at[1], r_ref, local_sem.at[1])
        load_x.start()
        load_r.start()
        gains = head_gains(gains_ref)
        gn = gains[0:1, :]
        pl.semaphore_wait(
            barrier, 2 * HEADS - 1 + (col > 0).astype(jnp.int32) + (col < cols - 1).astype(jnp.int32)
        )

        def term_copy(side, part):
            lines = pl.ds(part * span, span)
            return remote(
                (left_far if side == 0 else right_far).at[lines], from_ref.at[side, lines],
                t_send.at[side, part], t_recv.at[side, part],
                {"col": col - 1} if side == 0 else {"col": col + 1},
            )

        for part in range(PARTS):
            @pl.when(col > 0)
            def _():
                term_copy(0, part).start()

            @pl.when(col < cols - 1)
            def _():
                term_copy(1, part).start()

        load_x.wait()
        load_r.wait()
        for part in range(PARTS):
            @pl.when(col < cols - 1)
            def _():
                term_copy(0, part).wait_recv()

            @pl.when(col > 0)
            def _():
                term_copy(1, part).wait_recv()

            def total(row, carry):
                dnormed = own_ref[row]
                dnormed = dnormed + jnp.where(col < cols - 1, from_ref[0, row], 0.0)
                dnormed = dnormed + jnp.where(col > 0, from_ref[1, row], 0.0)
                scaled = dnormed * gn
                scaled_ref[row] = scaled
                product = (x_ref[row].astype(F32) * scaled).T
                mean_ref[pl.ds(row, 1), :] = jnp.sum(product, axis=0, keepdims=True)
                return carry

            lax.fori_loop(part * span, (part + 1) * span, total, 0)

        def mean_copy(src, dst):
            return remote(
                mean_ref, means_ref.at[src], m_send.at[dst], m_recv.at[src], {"row": dst}
            )

        def to(hop):
            return lax.rem(me + hop, HEADS)

        def back(hop):
            return lax.rem(me + HEADS - hop, HEADS)

        def start_mean(hop, carry):
            mean_copy(me, to(hop)).start()
            return carry

        def wait_mean(hop, carry):
            mean_copy(back(hop), me).wait_recv()
            return carry

        lax.fori_loop(1, HEADS, start_mean, 0)
        means_ref[me] = mean_ref[...]
        lax.fori_loop(1, HEADS, wait_mean, 0)
        mean_all = jnp.sum(means_ref[...], axis=0) / width
        means_ref[0] = mean_all

        def finish(row, carry):
            inverse = jnp.broadcast_to(r_ref[row, 0:1, :], (area, area))
            cube = inverse * inverse * inverse
            pull = (cube * means_ref[0, pl.ds(row, 1), :]).T
            grad = (
                cot_ref[row].astype(F32)
                + inverse.T * scaled_ref[row]
                - x_ref[row].astype(F32) * pull
            )
            grad_ref[row] = grad.astype(BF16)

            @pl.when(row > 0)
            def _():
                grad_copy(me, row - 1).start()

            return carry

        lax.fori_loop(0, rows, finish, 0)
        grad_copy(me, rows - 1).start()

    @pl.when(pipe == pipes - 1)
    def _():
        out_ref[...] = jnp.zeros_like(out_ref)

    @pl.when(pipe < pipes - 1)
    def _():
        def wait_grad(row, carry):
            remote(
                grad_ref.at[0], out_ref.at[:, head_lanes(row)], g_send.at[0], g_recv.at[row],
                {"pipe": pipe + 1, "row": row},
            ).wait_recv()
            return carry

        lax.fori_loop(0, rows, wait_grad, 0)

    @pl.when(pipe > 0)
    def _():
        def drain(row, carry):
            grad_copy(me, row).wait_send()
            return carry

        lax.fori_loop(0, rows, drain, 0)

        def drain_mean(hop, carry):
            dst = lax.rem(me + hop, HEADS)
            remote(
                mean_ref, means_ref.at[me], m_send.at[dst], m_recv.at[me], {"row": dst}
            ).wait_send()
            return carry

        lax.fori_loop(1, HEADS, drain_mean, 0)
        for part in range(PARTS):
            lines = pl.ds(part * span, span)

            @pl.when(col > 0)
            def _():
                remote(
                    left_far.at[lines], from_ref.at[0, lines], t_send.at[0, part],
                    t_recv.at[0, part], {"col": col - 1},
                ).wait_send()

            @pl.when(col < cols - 1)
            def _():
                remote(
                    right_far.at[lines], from_ref.at[1, lines], t_send.at[1, part],
                    t_recv.at[1, part], {"col": col + 1},
                ).wait_send()


def scatter(own, left, right, x3, r3, cot, gains):
    rows, area, depth = own.shape
    far = pl.BlockSpec(memory_space=pl.ANY)
    vmem = pl.BlockSpec(memory_space=pltpu.VMEM)
    dma = pltpu.SemaphoreType.DMA
    return pl.pallas_call(
        scatter_kernel,
        out_shape=jax.ShapeDtypeStruct((area, rows * depth), BF16),
        in_specs=[vmem, far, far, far, far, vmem, vmem],
        out_specs=vmem,
        scratch_shapes=[
            pltpu.VMEM((rows, area, depth), BF16),
            pltpu.VMEM((rows, 8, area), F32),
            pltpu.VMEM((2, rows, area, depth), F32),
            pltpu.VMEM((rows, area, depth), F32),
            pltpu.VMEM((rows, area), F32),
            pltpu.VMEM((HEADS, rows, area), F32),
            pltpu.VMEM((rows, area, depth), BF16),
            dma((2,)),
            dma((2, PARTS)), dma((2, PARTS)),
            dma((HEADS,)), dma((HEADS,)), dma((HEADS,)), dma((HEADS,)),
        ],
        compiler_params=pltpu.CompilerParams(collective_id=1, has_side_effects=True),
        name="finish_and_return",
    )(own, left, right, x3, r3, cot, gains)


def per_device(saved_in, cotangent, section_gains):
    _, tall, across, width = saved_in.shape
    area = tall * across
    gains = section_gains[0]
    x3, r3, cot = gather(saved_in.reshape(area, width), cotangent.reshape(area, width))
    own, left, right = attention(x3, r3, cot, gains)
    grad = scatter(own, left, right, x3, r3, cot, gains)
    return grad.reshape(1, tall, across, width)


def solution(mesh):
    return jax.shard_map(
        per_device,
        mesh=mesh,
        in_specs=(
            P("pipe", "row", "col", None),
            P("pipe", "row", "col", None),
            P("pipe", None, None),
        ),
        out_specs=P("pipe", "row", "col", None),
        check_vma=False,
    )
```

```python
import math

import jax
import jax.numpy as jnp
from jax import lax
from jax.experimental import pallas as pl
from jax.experimental.pallas import tpu as pltpu
from jax.sharding import PartitionSpec as P

HEADS = 16
HEAD_DIM = 128
TILE = 8
SPAN = 5
REACH = SPAN // 2
TERMS_LAG = 2
MEAN_LAG = 4

NEGATIVE = -1e30
EPSILON = 1e-06
F32 = jnp.float32
BF16 = jnp.bfloat16
MESH = pl.DeviceIdType.MESH


def dot(left, right, dims):
    return lax.dot_general(left, right, (dims, ((), ())), preferred_element_type=F32)


def fold(block, op):
    rows, lanes = block.shape
    return op(block.reshape(rows // 8, 8, lanes), axis=0)


def head_lanes(head):
    return pl.ds(pl.multiple_of(head * HEAD_DIM, HEAD_DIM), HEAD_DIM)


def remote(src, dst, send, recv, device):
    return pltpu.make_async_remote_copy(
        src_ref=src, dst_ref=dst, send_sem=send, recv_sem=recv,
        device_id=device, device_id_type=MESH,
    )


def loop(low, high, step):
    def body(index, carry):
        step(index)
        return carry

    lax.fori_loop(low, high, body, 0)


def section_kernel(
    x_ref, x_far, cot_far, gains_far, out_ref,
    x3_ref, r3_ref, cot_ref, gains_ref, inv_ref, bias_ref, kv_ref, kt_ref, qd_ref, w_ref,
    p_ref, dp_ref, own_ref, term_ref, from_ref, part_ref, mean_ref, grad_ref,
    local_sem, x_send, x_recv, r_send, r_recv, c_send, c_recv,
    fx_send, fx_recv, fr_send, fr_recv, t_send, t_recv, m_local, m_send, m_recv, g_send, g_recv,
):
    area = x_ref.shape[0]
    rows = HEADS
    depth = HEAD_DIM
    wide = 3 * area
    me = lax.axis_index("row")
    col = lax.axis_index("col")
    cols = lax.axis_size("col")
    pipe = lax.axis_index("pipe")
    pipes = lax.axis_size("pipe")
    has_left = col > 0
    has_right = col < cols - 1
    barrier = pltpu.get_barrier_semaphore()

    def greet(device):
        pl.semaphore_signal(barrier, inc=1, device_id=device, device_id_type=MESH)

    def to(hop):
        return lax.rem(me + hop, HEADS)

    def back(hop):
        return lax.rem(me + HEADS - hop, HEADS)

    def both(act):
        @pl.when(has_left)
        def _():
            act(0)

        @pl.when(has_right)
        def _():
            act(1)

    def side_device(side):
        return {"col": col - 1} if side == 0 else {"col": col + 1}

    def x_copy(src, dst):
        return remote(
            x_far.at[:, head_lanes(dst)], x3_ref.at[1, src], x_send.at[dst], x_recv.at[src],
            {"row": dst},
        )

    def r_copy(src, dst):
        return remote(inv_ref, r3_ref.at[1, src], r_send.at[dst], r_recv.at[src], {"row": dst})

    def c_copy(src, dst):
        return remote(
            cot_far.at[:, head_lanes(dst)], cot_ref.at[src], c_send.at[dst], c_recv.at[src],
            {"row": dst},
        )

    def fx_copy(src, side):
        return remote(
            x3_ref.at[1, src], x3_ref.at[2 - 2 * side, src], fx_send.at[side, src],
            fx_recv.at[side, src], side_device(side),
        )

    def fr_copy(src, side):
        return remote(
            r3_ref.at[1, src], r3_ref.at[2 - 2 * side, src], fr_send.at[side, src],
            fr_recv.at[side, src], side_device(side),
        )

    def t_copy(row, side):
        return remote(
            term_ref.at[side, row], from_ref.at[side, row], t_send.at[side, row],
            t_recv.at[side, row], side_device(side),
        )

    def m_copy(row, src, dst):
        return remote(
            part_ref.at[pl.ds(row, 1)], mean_ref.at[row, pl.ds(src, 1)],
            m_send.at[row, dst], m_recv.at[row, src], {"row": dst},
        )

    def g_copy(src, dst):
        return remote(
            grad_ref.at[dst], out_ref.at[:, head_lanes(src)], g_send.at[dst], g_recv.at[src],
            {"pipe": pipe - 1, "row": dst},
        )

    def work():
        loop(1, HEADS, lambda hop: greet({"row": to(hop)}))
        both(lambda side: greet(side_device(side)))
        local = [
            pltpu.make_async_copy(x_far.at[:, head_lanes(me)], x3_ref.at[1, me], local_sem.at[0]),
            pltpu.make_async_copy(cot_far.at[:, head_lanes(me)], cot_ref.at[me], local_sem.at[1]),
            pltpu.make_async_copy(gains_far.at[:, :, head_lanes(me)], gains_ref, local_sem.at[2]),
        ]
        for copy in local:
            copy.start()
        x_float = x_ref[...].astype(F32)
        square = jnp.mean(x_float * x_float, axis=-1, keepdims=True)
        inverse = jnp.broadcast_to(lax.rsqrt(square + EPSILON), (area, area))
        inv_ref[...] = inverse.T[:8]

        key = lax.broadcasted_iota(jnp.int32, (wide, area), 0)
        query = lax.broadcasted_iota(jnp.int32, (wide, area), 1)
        key_tile = 2 * (key // area) + (key // TILE) % 2
        query_tile = (query // TILE) % 2
        near = (key_tile >= query_tile) & (key_tile <= query_tile + 2 * REACH)
        inside = (col * 2 + key_tile >= REACH) & (col * 2 + key_tile < 2 * cols + REACH)
        bias_ref[0] = jnp.full((wide, area), NEGATIVE, F32)
        bias_ref[1] = jnp.where(near & inside, 0.0, NEGATIVE)
        for pad in (0, 1, rows + 2, rows + 3):
            kv_ref[pad] = jnp.zeros((wide, 2 * depth), BF16)
            kt_ref[pad] = jnp.zeros((depth, wide), BF16)
            qd_ref[pad] = jnp.zeros((2 * area, 2 * depth), BF16)
        for key_line, slot in ((0, 0), (0, 1), (1, 0), (rows - 2, 4), (rows - 1, 3), (rows - 1, 4)):
            w_ref[key_line + REACH, :, slot * 2 * area : (slot + 1) * 2 * area] = jnp.zeros(
                (wide, 2 * area), BF16
            )
        pl.semaphore_wait(
            barrier, 2 * HEADS - 1 + has_left.astype(jnp.int32) + has_right.astype(jnp.int32)
        )

        loop(1, HEADS, lambda hop: x_copy(me, to(hop)).start())
        loop(1, HEADS, lambda hop: r_copy(me, to(hop)).start())
        own_r = pltpu.make_async_copy(inv_ref, r3_ref.at[1, me], local_sem.at[3])
        own_r.start()
        loop(1, HEADS, lambda hop: c_copy(me, to(hop)).start())
        for copy in local:
            copy.wait()
        own_r.wait()

        gn = gains_ref[0]
        gq = gains_ref[1] * (1.0 / math.sqrt(HEAD_DIM))
        gk = gains_ref[2]
        gv = gains_ref[3]
        go = gains_ref[4]

        def prepare(row, block):
            inverse = jnp.broadcast_to(r3_ref[block, row, 0:1, :], (area, area)).T
            x_float = x3_ref[block, row].astype(F32)
            normed = (x_float * inverse * gn).astype(BF16).astype(F32)
            keys = (normed * gk).astype(BF16)
            lanes = slice(block * area, (block + 1) * area)
            kv_ref[row + REACH, lanes, :depth] = keys
            kv_ref[row + REACH, lanes, depth:] = (normed * gv).astype(BF16)
            kt_ref[row + REACH, :, lanes] = keys.T
            if block == 1:
                qd_ref[row + REACH, :area, :depth] = (normed * gq).astype(BF16)
                qd_ref[row + REACH, :area, depth:] = jnp.zeros((area, depth), BF16)
                qd_ref[row + REACH, area:, :depth] = jnp.zeros((area, depth), BF16)

        def pass_on(src):
            both(lambda side: fx_copy(src, side).start())
            both(lambda side: fr_copy(src, side).start())
            prepare(src, 1)

        pass_on(me)

        def arrive(hop):
            src = back(hop)
            x_copy(src, me).wait_recv()
            r_copy(src, me).wait_recv()
            pass_on(src)

        loop(1, HEADS, arrive)

        def beside(hop):
            src = back(hop)
            for block, side in ((2, 0), (0, 1)):
                present = has_left if block == 0 else has_right
                lanes = slice(block * area, (block + 1) * area)

                @pl.when(present)
                def _():
                    fx_copy(src, side).wait_recv()
                    fr_copy(src, side).wait_recv()
                    prepare(src, block)

                @pl.when(jnp.logical_not(present))
                def _():
                    kv_ref[src + REACH, lanes, :] = jnp.zeros((area, 2 * depth), BF16)
                    kt_ref[src + REACH, :, lanes] = jnp.zeros((depth, area), BF16)

        loop(0, HEADS, beside)

        def soften(row):
            queries = qd_ref[row + REACH, :area, :depth]
            top = jnp.full((8, area), NEGATIVE, F32)
            for off in range(SPAN):
                far = row + off - REACH
                valid = jnp.logical_and(far >= 0, far < rows).astype(jnp.int32)
                scores = dot(kv_ref[row + off, :, :depth], queries, ((1,), (1,))) + bias_ref[valid]
                p_ref[row, off] = scores
                top = jnp.maximum(top, fold(scores, jnp.max))
            top = jnp.max(top, axis=0, keepdims=True)
            total = jnp.zeros((8, area), F32)
            for off in range(SPAN):
                raised = jnp.exp(p_ref[row, off] - top)
                p_ref[row, off] = raised
                total = total + fold(raised, jnp.sum)
            scale = 1.0 / jnp.sum(total, axis=0, keepdims=True)
            for off in range(SPAN):
                weights = p_ref[row, off] * scale
                p_ref[row, off] = weights
                slot = SPAN - 1 - off
                w_ref[row + off, :, slot * 2 * area + area : (slot + 1) * 2 * area] = weights.astype(
                    BF16
                )

        loop(0, rows, soften)

        def upstream(hop):
            src = back(hop)

            @pl.when(hop > 0)
            def _():
                c_copy(src, me).wait_recv()

            qd_ref[src + REACH, area:, depth:] = (cot_ref[src].astype(F32) * go).astype(BF16)

        loop(0, HEADS, upstream)

        def grade(row):
            grads = qd_ref[row + REACH, area:, depth:]
            delta = jnp.zeros((8, area), F32)
            for off in range(SPAN):
                slot = SPAN - 1 - off
                product = dot(kv_ref[row + off, :, depth:], grads, ((1,), (1,)))
                dp_ref[off] = product
                rounded = w_ref[row + off, :, slot * 2 * area + area : (slot + 1) * 2 * area]
                delta = delta + fold(rounded.astype(F32) * product, jnp.sum)
            delta = jnp.sum(delta, axis=0, keepdims=True)
            turned = jnp.zeros((depth, area), F32)
            for off in range(SPAN):
                slot = SPAN - 1 - off
                dscore = (p_ref[row, off] * (dp_ref[off] - delta)).astype(BF16)
                w_ref[row + off, :, slot * 2 * area : slot * 2 * area + area] = dscore
                turned = turned + dot(kt_ref[row + off], dscore, ((1,), (0,)))
            own_ref[row] = turned.T * gq

        def key_line(row):
            pairs = qd_ref[pl.ds(row, SPAN)].reshape(SPAN * 2 * area, 2 * depth)
            grads = dot(w_ref[row + REACH], pairs, ((1,), (0,)))
            terms = grads[:, :depth] * gk + grads[:, depth:] * gv
            term_ref[0, row] = terms[:area]
            own_ref[row] = own_ref[row] + terms[area : 2 * area]
            term_ref[1, row] = terms[2 * area :]

        def collect(row):
            both(lambda side: t_copy(row, 1 - side).wait_recv())
            dnormed = own_ref[row]
            dnormed = dnormed + jnp.where(has_right, from_ref[0, row], 0.0)
            dnormed = dnormed + jnp.where(has_left, from_ref[1, row], 0.0)
            scaled = dnormed * gn
            own_ref[row] = scaled
            product = (x3_ref[1, row].astype(F32) * scaled).T
            part_ref[pl.ds(row, 1), :] = jnp.sum(product, axis=0, keepdims=True)

        def own_part(row):
            return pltpu.make_async_copy(
                part_ref.at[pl.ds(row, 1)], mean_ref.at[row, pl.ds(me, 1)], m_local.at[row]
            )

        def share(row):
            own_part(row).start()
            loop(1, HEADS, lambda hop: m_copy(row, me, to(hop)).start())

        def close(row):
            own_part(row).wait()
            loop(1, HEADS, lambda hop: m_copy(row, back(hop), me).wait_recv())
            mean = jnp.sum(mean_ref[row], axis=0, keepdims=True) / (rows * depth)
            inverse = jnp.broadcast_to(r3_ref[1, row, 0:1, :], (area, area))
            pull = (inverse * inverse * inverse * mean).T
            grad = (
                cot_ref[row].astype(F32)
                + inverse.T * own_ref[row]
                - x3_ref[1, row].astype(F32) * pull
            )
            grad_ref[row] = grad.astype(BF16)

        stages = (
            (grade, 0),
            (key_line, REACH),
            (lambda row: both(lambda side: t_copy(row, side).start()), REACH + 1),
            (collect, REACH + 1 + TERMS_LAG),
            (share, REACH + 2 + TERMS_LAG),
            (close, REACH + 2 + TERMS_LAG + MEAN_LAG),
            (lambda row: g_copy(me, row).start(), REACH + 3 + TERMS_LAG + MEAN_LAG),
        )

        def advance(step):
            for act, lag in stages:
                @pl.when(jnp.logical_and(step >= lag, step < rows + lag))
                def _():
                    act(step - lag)

        loop(0, rows + stages[-1][1], advance)

    @pl.when(pipe < pipes - 1)
    def _():
        loop(0, rows, lambda row: greet({"pipe": pipe + 1, "row": row}))

    @pl.when(pipe == pipes - 1)
    def _():
        out_ref[...] = jnp.zeros_like(out_ref)

    @pl.when(pipe > 0)
    def _():
        work()

    @pl.when(pipe < pipes - 1)
    def _():
        def wait_grad(row):
            remote(
                grad_ref.at[0], out_ref.at[:, head_lanes(row)], g_send.at[0], g_recv.at[row],
                {"pipe": pipe + 1, "row": row},
            ).wait_recv()

        loop(0, rows, wait_grad)

    @pl.when(pipe > 0)
    def _():
        def drain(hop):
            x_copy(me, to(hop)).wait_send()
            r_copy(me, to(hop)).wait_send()
            c_copy(me, to(hop)).wait_send()

        loop(1, HEADS, drain)

        def drain_row(row):
            both(lambda side: fx_copy(row, side).wait_send())
            both(lambda side: fr_copy(row, side).wait_send())
            both(lambda side: t_copy(row, side).wait_send())
            loop(1, HEADS, lambda hop: m_copy(row, me, to(hop)).wait_send())
            g_copy(me, row).wait_send()

        loop(0, rows, drain_row)


def per_device(saved_in, cotangent, section_gains):
    _, tall, across, width = saved_in.shape
    area = tall * across
    rows = HEADS
    wide = 3 * area
    x = saved_in.reshape(area, width)
    cot = cotangent.reshape(area, width)
    gains = section_gains.transpose(1, 0, 2)
    far = pl.BlockSpec(memory_space=pl.ANY)
    vmem = pl.BlockSpec(memory_space=pltpu.VMEM)
    dma = pltpu.SemaphoreType.DMA
    grad = pl.pallas_call(
        section_kernel,
        out_shape=jax.ShapeDtypeStruct((area, width), BF16),
        in_specs=[vmem, far, far, far],
        out_specs=vmem,
        scratch_shapes=[
            pltpu.VMEM((3, rows, area, HEAD_DIM), BF16),
            pltpu.VMEM((3, rows, 8, area), F32),
            pltpu.VMEM((rows, area, HEAD_DIM), BF16),
            pltpu.VMEM((gains.shape[0], 1, HEAD_DIM), F32),
            pltpu.VMEM((8, area), F32),
            pltpu.VMEM((2, wide, area), F32),
            pltpu.VMEM((rows + 4, wide, 2 * HEAD_DIM), BF16),
            pltpu.VMEM((rows + 4, HEAD_DIM, wide), BF16),
            pltpu.VMEM((rows + 4, 2 * area, 2 * HEAD_DIM), BF16),
            pltpu.VMEM((rows + 4, wide, SPAN * 2 * area), BF16),
            pltpu.VMEM((rows, SPAN, wide, area), F32),
            pltpu.VMEM((SPAN, wide, area), F32),
            pltpu.VMEM((rows, area, HEAD_DIM), F32),
            pltpu.VMEM((2, rows, area, HEAD_DIM), F32),
            pltpu.VMEM((2, rows, area, HEAD_DIM), F32),
            pltpu.VMEM((rows, area), F32),
            pltpu.VMEM((rows, HEADS, area), F32),
            pltpu.VMEM((rows, area, HEAD_DIM), BF16),
            dma((4,)),
            dma((HEADS,)), dma((HEADS,)), dma((HEADS,)), dma((HEADS,)), dma((HEADS,)), dma((HEADS,)),
            dma((2, HEADS)), dma((2, HEADS)), dma((2, HEADS)), dma((2, HEADS)),
            dma((2, rows)), dma((2, rows)),
            dma((rows,)), dma((rows, HEADS)), dma((rows, HEADS)),
            dma((rows,)), dma((HEADS,)),
        ],
        compiler_params=pltpu.CompilerParams(
            collective_id=0, has_side_effects=True, vmem_limit_bytes=60 * 1024 * 1024
        ),
        name="section_backward",
    )(x, x, cot, gains)
    return grad.reshape(1, tall, across, width)


def solution(mesh):
    return jax.shard_map(
        per_device,
        mesh=mesh,
        in_specs=(
            P("pipe", "row", "col", None),
            P("pipe", "row", "col", None),
            P("pipe", None, None),
        ),
        out_specs=P("pipe", "row", "col", None),
        check_vma=False,
    )
```

```python
import functools
import math

import jax
import jax.numpy as jnp
from jax import lax
from jax.experimental import pallas as pl
from jax.experimental.pallas import tpu as pltpu
from jax.sharding import PartitionSpec as P

HEADS = 16
HEAD_DIM = 128
TILE = 8
SPAN = 5
REACH = SPAN // 2
GROUP = 4
TERMS_LAG = 1
MEAN_LAG = 7

NEGATIVE = -1e30
EPSILON = 1e-06
F32 = jnp.float32
BF16 = jnp.bfloat16
MESH = pl.DeviceIdType.MESH


def dot(left, right, dims):
    return lax.dot_general(left, right, (dims, ((), ())), preferred_element_type=F32)


def fold(block, op):
    rows, lanes = block.shape
    return op(block.reshape(rows // 8, 8, lanes), axis=0)


def head_lanes(head):
    return pl.ds(pl.multiple_of(head * HEAD_DIM, HEAD_DIM), HEAD_DIM)


def remote(src, dst, send, recv, device):
    return pltpu.make_async_remote_copy(
        src_ref=src, dst_ref=dst, send_sem=send, recv_sem=recv,
        device_id=device, device_id_type=MESH,
    )


def loop(low, high, step):
    def body(index, carry):
        step(index)
        return carry

    lax.fori_loop(low, high, body, 0)


def section_kernel(
    x_ref, x_far, cot_far, gains_far, out_ref,
    x3_ref, r3_ref, cot_ref, gains_ref, inv_ref, bias_ref, kv_ref, kt_ref, qd_ref, w_ref,
    p_ref, scale_ref, dp_ref, own_ref, term_ref, from_ref, part_ref, mean_ref, grad_ref,
    local_sem, x_send, x_recv, r_send, r_recv, c_send, c_recv,
    fx_send, fx_recv, fr_send, fr_recv, t_send, t_recv, m_local, m_send, m_recv, g_send, g_recv,
):
    area = x_ref.shape[0]
    rows = HEADS
    depth = HEAD_DIM
    wide = 3 * area
    me = lax.axis_index("row")
    col = lax.axis_index("col")
    cols = lax.axis_size("col")
    pipe = lax.axis_index("pipe")
    pipes = lax.axis_size("pipe")
    has_left = col > 0
    has_right = col < cols - 1
    barrier = pltpu.get_barrier_semaphore()

    def greet(device):
        pl.semaphore_signal(barrier, inc=1, device_id=device, device_id_type=MESH)

    def to(hop):
        return lax.rem(me + hop, HEADS)

    def back(hop):
        return lax.rem(me + HEADS - hop, HEADS)

    def both(act):
        @pl.when(has_left)
        def _():
            act(0)

        @pl.when(has_right)
        def _():
            act(1)

    def side_device(side):
        return {"col": col - 1} if side == 0 else {"col": col + 1}

    def x_copy(src, dst):
        return remote(
            x_far.at[:, head_lanes(dst)], x3_ref.at[1, src], x_send.at[dst], x_recv.at[src],
            {"row": dst},
        )

    def r_copy(src, dst):
        return remote(inv_ref, r3_ref.at[1, src], r_send.at[dst], r_recv.at[src], {"row": dst})

    def c_copy(src, dst):
        return remote(
            cot_far.at[:, head_lanes(dst)], cot_ref.at[src], c_send.at[dst], c_recv.at[src],
            {"row": dst},
        )

    def fx_copy(src, side):
        return remote(
            x3_ref.at[1, src], x3_ref.at[2 - 2 * side, src], fx_send.at[side, src],
            fx_recv.at[side, src], side_device(side),
        )

    def fr_copy(src, side):
        return remote(
            r3_ref.at[1, src], r3_ref.at[2 - 2 * side, src], fr_send.at[side, src],
            fr_recv.at[side, src], side_device(side),
        )

    def t_copy(row, side):
        return remote(
            term_ref.at[side, row], from_ref.at[side, row], t_send.at[side, row],
            t_recv.at[side, row], side_device(side),
        )

    def m_copy(group, src, dst):
        return remote(
            part_ref.at[group], mean_ref.at[group, src],
            m_send.at[group, dst], m_recv.at[group, src], {"row": dst},
        )

    def g_copy(src, dst):
        return remote(
            grad_ref.at[dst], out_ref.at[:, head_lanes(src)], g_send.at[dst], g_recv.at[src],
            {"pipe": pipe - 1, "row": dst},
        )

    def work():
        loop(1, HEADS, lambda hop: greet({"row": to(hop)}))
        both(lambda side: greet(side_device(side)))
        local = [
            pltpu.make_async_copy(x_far.at[:, head_lanes(me)], x3_ref.at[1, me], local_sem.at[0]),
            pltpu.make_async_copy(cot_far.at[:, head_lanes(me)], cot_ref.at[me], local_sem.at[1]),
            pltpu.make_async_copy(gains_far.at[:, :, head_lanes(me)], gains_ref, local_sem.at[2]),
        ]
        for copy in local:
            copy.start()
        x_float = x_ref[...].astype(F32)
        square = jnp.mean(x_float * x_float, axis=-1, keepdims=True)
        inverse = jnp.broadcast_to(lax.rsqrt(square + EPSILON), (area, area))
        inv_ref[...] = inverse.T[:1]

        key = lax.broadcasted_iota(jnp.int32, (wide, area), 0)
        query = lax.broadcasted_iota(jnp.int32, (wide, area), 1)
        key_tile = 2 * (key // area) + (key // TILE) % 2
        query_tile = (query // TILE) % 2
        near = (key_tile >= query_tile) & (key_tile <= query_tile + 2 * REACH)
        inside = (col * 2 + key_tile >= REACH) & (col * 2 + key_tile < 2 * cols + REACH)
        bias_ref[0] = jnp.full((wide, area), NEGATIVE, F32)
        bias_ref[1] = jnp.where(near & inside, 0.0, NEGATIVE)
        for pad in (0, 1, rows + 2, rows + 3):
            kv_ref[pad] = jnp.zeros((wide, 2 * depth), BF16)
            kt_ref[pad] = jnp.zeros((depth, wide), BF16)
            qd_ref[pad] = jnp.zeros((2 * area, 2 * depth), BF16)
        for key_line, slot in ((0, 0), (0, 1), (1, 0), (rows - 2, 4), (rows - 1, 3), (rows - 1, 4)):
            w_ref[key_line + REACH, :, slot * 2 * area : (slot + 1) * 2 * area] = jnp.zeros(
                (wide, 2 * area), BF16
            )
        pl.semaphore_wait(
            barrier, 2 * HEADS - 1 + has_left.astype(jnp.int32) + has_right.astype(jnp.int32)
        )

        loop(1, HEADS, lambda hop: r_copy(me, to(hop)).start())
        loop(1, HEADS, lambda hop: x_copy(me, to(hop)).start())
        own_r = pltpu.make_async_copy(inv_ref, r3_ref.at[1, me], local_sem.at[3])
        own_r.start()
        loop(1, HEADS, lambda hop: c_copy(me, to(hop)).start())
        for copy in local:
            copy.wait()
        own_r.wait()

        gn = gains_ref[0]
        gq = gains_ref[1] * (1.0 / math.sqrt(HEAD_DIM))
        gk = gains_ref[2]
        gv = gains_ref[3]
        go = gains_ref[4]

        def prepare(row, block):
            inverse = jnp.broadcast_to(r3_ref[block, row], (area, area)).T
            x_float = x3_ref[block, row].astype(F32)
            normed = (x_float * inverse * gn).astype(BF16).astype(F32)
            keys = (normed * gk).astype(BF16)
            lanes = slice(block * area, (block + 1) * area)
            kv_ref[row + REACH, lanes, :depth] = keys
            kv_ref[row + REACH, lanes, depth:] = (normed * gv).astype(BF16)
            kt_ref[row + REACH, :, lanes] = keys.T
            if block == 1:
                qd_ref[row + REACH, :area, :depth] = (normed * gq).astype(BF16)
                qd_ref[row + REACH, :area, depth:] = jnp.zeros((area, depth), BF16)
                qd_ref[row + REACH, area:, :depth] = jnp.zeros((area, depth), BF16)

        def pass_on(src):
            both(lambda side: fx_copy(src, side).start())
            both(lambda side: fr_copy(src, side).start())
            prepare(src, 1)

        pass_on(me)

        def arrive(hop):
            src = back(hop)
            x_copy(src, me).wait_recv()
            r_copy(src, me).wait_recv()
            pass_on(src)

        loop(1, HEADS, arrive)

        def await_beside(src, side):
            fx_copy(src, side).wait_recv()
            fr_copy(src, side).wait_recv()

        def blank(src, block):
            lanes = slice(block * area, (block + 1) * area)
            kv_ref[src + REACH, lanes, :] = jnp.zeros((area, 2 * depth), BF16)
            kt_ref[src + REACH, :, lanes] = jnp.zeros((depth, area), BF16)

        def beside(pair):
            sources = (back(2 * pair), back(2 * pair + 1))

            @pl.when(jnp.logical_and(has_left, has_right))
            def _():
                for src in sources:
                    await_beside(src, 0)
                    await_beside(src, 1)
                for src in sources:
                    prepare(src, 0)
                    prepare(src, 2)

            @pl.when(jnp.logical_not(has_left))
            def _():
                for src in sources:
                    await_beside(src, 0)
                for src in sources:
                    prepare(src, 2)
                    blank(src, 0)

            @pl.when(jnp.logical_not(has_right))
            def _():
                for src in sources:
                    await_beside(src, 1)
                for src in sources:
                    prepare(src, 0)
                    blank(src, 2)

        loop(0, HEADS // 2, beside)

        def lines_of(block):
            return slice(block * area, (block + 1) * area)

        def soften(row):
            queries = qd_ref[row + REACH, :area, :depth]
            tops = []
            totals = []
            for off in range(SPAN):
                far = row + off - REACH
                valid = jnp.logical_and(far >= 0, far < rows)
                index = valid.astype(jnp.int32)
                for block in range(3):
                    lines = lines_of(block)
                    scores = dot(kv_ref[row + off, lines, :depth], queries, ((1,), (1,)))
                    if block == 1:
                        scores = scores + jnp.where(valid, 0.0, NEGATIVE)
                    else:
                        scores = scores + bias_ref[index, lines, :]
                    top = jnp.max(fold(scores, jnp.max), axis=0, keepdims=True)
                    raised = jnp.exp(scores - top)
                    p_ref[row, off, lines, :] = raised
                    tops.append(top)
                    totals.append(fold(raised, jnp.sum))
            peak = functools.reduce(jnp.maximum, tops)
            shares = [jnp.exp(top - peak) for top in tops]
            total = jnp.sum(sum(t * f for t, f in zip(totals, shares)), axis=0, keepdims=True)
            inverse = 1.0 / total
            for index, share in enumerate(shares):
                scale_ref[row, index : index + 1, :] = share * inverse

        loop(0, rows, soften)

        def upstream(hop):
            src = back(hop)

            @pl.when(hop > 0)
            def _():
                c_copy(src, me).wait_recv()

            qd_ref[src + REACH, area:, depth:] = (cot_ref[src].astype(F32) * go).astype(BF16)

        loop(0, HEADS, upstream)

        def grade(row):
            grads = qd_ref[row + REACH, area:, depth:]
            delta = jnp.zeros((8, area), F32)
            for off in range(SPAN):
                slot = 2 * area * (SPAN - 1 - off)
                for block in range(3):
                    lines = lines_of(block)
                    index = 3 * off + block
                    product = dot(kv_ref[row + off, lines, depth:], grads, ((1,), (1,)))
                    dp_ref[off, lines, :] = product
                    weights = p_ref[row, off, lines, :] * scale_ref[row, index : index + 1, :]
                    rounded = weights.astype(BF16)
                    w_ref[row + off, lines, slot + area : slot + 2 * area] = rounded
                    delta = delta + fold(rounded.astype(F32) * product, jnp.sum)
            delta = jnp.sum(delta, axis=0, keepdims=True)
            turned = jnp.zeros((depth, area), F32)
            for off in range(SPAN):
                slot = 2 * area * (SPAN - 1 - off)
                pieces = []
                for block in range(3):
                    lines = lines_of(block)
                    index = 3 * off + block
                    weights = p_ref[row, off, lines, :] * scale_ref[row, index : index + 1, :]
                    dscore = (weights * (dp_ref[off, lines, :] - delta)).astype(BF16)
                    w_ref[row + off, lines, slot : slot + area] = dscore
                    pieces.append(dscore)
                dscore = jnp.concatenate(pieces, axis=0)
                turned = turned + dot(kt_ref[row + off], dscore, ((1,), (0,)))
            own_ref[row] = turned.T * gq

        def key_line(row):
            pairs = qd_ref[pl.ds(row, SPAN)].reshape(SPAN * 2 * area, 2 * depth)
            grads = dot(w_ref[row + REACH], pairs, ((1,), (0,)))
            terms = grads[:, :depth] * gk + grads[:, depth:] * gv
            term_ref[0, row] = terms[:area]
            own_ref[row] = own_ref[row] + terms[area : 2 * area]
            term_ref[1, row] = terms[2 * area :]

        def collect(row):
            both(lambda side: t_copy(row, 1 - side).wait_recv())
            dnormed = own_ref[row]
            dnormed = dnormed + jnp.where(has_right, from_ref[0, row], 0.0)
            dnormed = dnormed + jnp.where(has_left, from_ref[1, row], 0.0)
            scaled = dnormed * gn
            own_ref[row] = scaled
            product = (x3_ref[1, row].astype(F32) * scaled).T
            part_ref[row // GROUP, pl.ds(row % GROUP, 1), :] = jnp.sum(
                product, axis=0, keepdims=True
            )

        def own_part(group):
            return pltpu.make_async_copy(
                part_ref.at[group], mean_ref.at[group, me], m_local.at[group]
            )

        def share(row):
            @pl.when(row % GROUP == GROUP - 1)
            def _():
                group = row // GROUP
                own_part(group).start()
                loop(1, HEADS, lambda hop: m_copy(group, me, to(hop)).start())

        def close(row):
            @pl.when(row % GROUP == GROUP - 1)
            def _():
                group = row // GROUP
                own_part(group).wait()
                loop(1, HEADS, lambda hop: m_copy(group, back(hop), me).wait_recv())
                means = jnp.sum(mean_ref[group], axis=0) / (rows * depth)
                for line in range(GROUP):
                    each = group * GROUP + line
                    inverse = jnp.broadcast_to(r3_ref[1, each], (area, area))
                    pull = (inverse * inverse * inverse * means[line : line + 1]).T
                    grad = (
                        cot_ref[each].astype(F32)
                        + inverse.T * own_ref[each]
                        - x3_ref[1, each].astype(F32) * pull
                    )
                    grad_ref[each] = grad.astype(BF16)

        def give_back(row):
            @pl.when(row % GROUP == GROUP - 1)
            def _():
                for line in range(GROUP):
                    g_copy(me, row - line).start()

        stages = (
            (grade, 0),
            (key_line, REACH),
            (lambda row: both(lambda side: t_copy(row, side).start()), REACH + 1),
            (collect, REACH + 1 + TERMS_LAG),
            (share, REACH + 2 + TERMS_LAG),
            (close, REACH + 2 + TERMS_LAG + MEAN_LAG),
            (give_back, REACH + 3 + TERMS_LAG + MEAN_LAG),
        )

        def advance(step):
            for act, lag in stages:
                @pl.when(jnp.logical_and(step >= lag, step < rows + lag))
                def _():
                    act(step - lag)

        loop(0, rows + stages[-1][1], advance)

    @pl.when(pipe < pipes - 1)
    def _():
        loop(0, rows, lambda row: greet({"pipe": pipe + 1, "row": row}))

    @pl.when(pipe == pipes - 1)
    def _():
        out_ref[...] = jnp.zeros_like(out_ref)

    @pl.when(pipe > 0)
    def _():
        work()

    @pl.when(pipe < pipes - 1)
    def _():
        def wait_grad(row):
            remote(
                grad_ref.at[0], out_ref.at[:, head_lanes(row)], g_send.at[0], g_recv.at[row],
                {"pipe": pipe + 1, "row": row},
            ).wait_recv()

        loop(0, rows, wait_grad)

    @pl.when(pipe > 0)
    def _():
        def drain(hop):
            x_copy(me, to(hop)).wait_send()
            r_copy(me, to(hop)).wait_send()
            c_copy(me, to(hop)).wait_send()

        loop(1, HEADS, drain)

        def drain_row(row):
            both(lambda side: fx_copy(row, side).wait_send())
            both(lambda side: fr_copy(row, side).wait_send())
            both(lambda side: t_copy(row, side).wait_send())
            g_copy(me, row).wait_send()

        loop(0, rows, drain_row)

        def drain_group(group):
            loop(1, HEADS, lambda hop: m_copy(group, me, to(hop)).wait_send())

        loop(0, rows // GROUP, drain_group)


def per_device(saved_in, cotangent, section_gains):
    _, tall, across, width = saved_in.shape
    area = tall * across
    rows = HEADS
    wide = 3 * area
    x = saved_in.reshape(area, width)
    cot = cotangent.reshape(area, width)
    gains = section_gains.transpose(1, 0, 2)
    far = pl.BlockSpec(memory_space=pl.ANY)
    vmem = pl.BlockSpec(memory_space=pltpu.VMEM)
    dma = pltpu.SemaphoreType.DMA
    grad = pl.pallas_call(
        section_kernel,
        out_shape=jax.ShapeDtypeStruct((area, width), BF16),
        in_specs=[vmem, far, far, far],
        out_specs=vmem,
        scratch_shapes=[
            pltpu.VMEM((3, rows, area, HEAD_DIM), BF16),
            pltpu.VMEM((3, rows, 1, area), F32),
            pltpu.VMEM((rows, area, HEAD_DIM), BF16),
            pltpu.VMEM((gains.shape[0], 1, HEAD_DIM), F32),
            pltpu.VMEM((1, area), F32),
            pltpu.VMEM((2, wide, area), F32),
            pltpu.VMEM((rows + 4, wide, 2 * HEAD_DIM), BF16),
            pltpu.VMEM((rows + 4, HEAD_DIM, wide), BF16),
            pltpu.VMEM((rows + 4, 2 * area, 2 * HEAD_DIM), BF16),
            pltpu.VMEM((rows + 4, wide, SPAN * 2 * area), BF16),
            pltpu.VMEM((rows, SPAN, wide, area), F32),
            pltpu.VMEM((rows, 3 * SPAN, area), F32),
            pltpu.VMEM((SPAN, wide, area), F32),
            pltpu.VMEM((rows, area, HEAD_DIM), F32),
            pltpu.VMEM((2, rows, area, HEAD_DIM), F32),
            pltpu.VMEM((2, rows, area, HEAD_DIM), F32),
            pltpu.VMEM((rows // GROUP, GROUP, area), F32),
            pltpu.VMEM((rows // GROUP, HEADS, GROUP, area), F32),
            pltpu.VMEM((rows, area, HEAD_DIM), BF16),
            dma((4,)),
            dma((HEADS,)), dma((HEADS,)), dma((HEADS,)), dma((HEADS,)), dma((HEADS,)), dma((HEADS,)),
            dma((2, HEADS)), dma((2, HEADS)), dma((2, HEADS)), dma((2, HEADS)),
            dma((2, rows)), dma((2, rows)),
            dma((rows // GROUP,)), dma((rows // GROUP, HEADS)), dma((rows // GROUP, HEADS)),
            dma((rows,)), dma((HEADS,)),
        ],
        compiler_params=pltpu.CompilerParams(
            collective_id=0, has_side_effects=True, vmem_limit_bytes=60 * 1024 * 1024
        ),
        name="section_backward",
    )(x, x, cot, gains)
    return grad.reshape(1, tall, across, width)


def solution(mesh):
    return jax.shard_map(
        per_device,
        mesh=mesh,
        in_specs=(
            P("pipe", "row", "col", None),
            P("pipe", "row", "col", None),
            P("pipe", None, None),
        ),
        out_specs=P("pipe", "row", "col", None),
        check_vma=False,
    )
```

```python
import functools
import math

import jax
import jax.numpy as jnp
from jax import lax
from jax.experimental import pallas as pl
from jax.experimental.pallas import tpu as pltpu
from jax.sharding import PartitionSpec as P

HEADS = 16
HEAD_DIM = 128
TILE = 8
SPAN = 5
REACH = SPAN // 2
GROUP = 4
TERMS_LAG = 1
MEAN_LAG = 6

NEGATIVE = -1e30
EPSILON = 1e-06
F32 = jnp.float32
BF16 = jnp.bfloat16
MESH = pl.DeviceIdType.MESH


def dot(left, right, dims):
    return lax.dot_general(left, right, (dims, ((), ())), preferred_element_type=F32)


def fold(block, op):
    rows, lanes = block.shape
    return op(block.reshape(rows // 8, 8, lanes), axis=0)


def head_lanes(head):
    return pl.ds(pl.multiple_of(head * HEAD_DIM, HEAD_DIM), HEAD_DIM)


def remote(src, dst, send, recv, device):
    return pltpu.make_async_remote_copy(
        src_ref=src, dst_ref=dst, send_sem=send, recv_sem=recv,
        device_id=device, device_id_type=MESH,
    )


def loop(low, high, step):
    def body(index, carry):
        step(index)
        return carry

    lax.fori_loop(low, high, body, 0)


def section_kernel(
    x_ref, x_far, cot_far, gains_far, out_ref,
    x3_ref, r3_ref, cot_ref, gains_ref, inv_ref, bias_ref, kv_ref, kt_ref, qd_ref, w_ref,
    p_ref, scale_ref, delta_ref, dp_ref, own_ref, term_ref, from_ref, part_ref, mean_ref, grad_ref,
    local_sem, x_send, x_recv, r_send, r_recv, c_send, c_recv,
    fx_send, fx_recv, fr_send, fr_recv, t_send, t_recv, m_local, m_send, m_recv, g_send, g_recv,
):
    area = x_ref.shape[0]
    rows = HEADS
    depth = HEAD_DIM
    wide = 3 * area
    me = lax.axis_index("row")
    col = lax.axis_index("col")
    cols = lax.axis_size("col")
    pipe = lax.axis_index("pipe")
    pipes = lax.axis_size("pipe")
    has_left = col > 0
    has_right = col < cols - 1
    barrier = pltpu.get_barrier_semaphore()

    def greet(device):
        pl.semaphore_signal(barrier, inc=1, device_id=device, device_id_type=MESH)

    def to(hop):
        return lax.rem(me + hop, HEADS)

    def back(hop):
        return lax.rem(me + HEADS - hop, HEADS)

    def both(act):
        @pl.when(has_left)
        def _():
            act(0)

        @pl.when(has_right)
        def _():
            act(1)

    def side_device(side):
        return {"col": col - 1} if side == 0 else {"col": col + 1}

    def x_copy(src, dst):
        return remote(
            x_far.at[:, head_lanes(dst)], x3_ref.at[1, src], x_send.at[dst], x_recv.at[src],
            {"row": dst},
        )

    def r_copy(src, dst):
        return remote(inv_ref, r3_ref.at[1, src], r_send.at[dst], r_recv.at[src], {"row": dst})

    def c_copy(src, dst):
        return remote(
            cot_far.at[:, head_lanes(dst)], cot_ref.at[src], c_send.at[dst], c_recv.at[src],
            {"row": dst},
        )

    def fx_copy(src, side):
        return remote(
            x3_ref.at[1, src], x3_ref.at[2 - 2 * side, src], fx_send.at[side, src],
            fx_recv.at[side, src], side_device(side),
        )

    def fr_copy(src, side):
        return remote(
            r3_ref.at[1, src], r3_ref.at[2 - 2 * side, src], fr_send.at[side, src],
            fr_recv.at[side, src], side_device(side),
        )

    def t_copy(row, side):
        return remote(
            term_ref.at[side, row], from_ref.at[side, row], t_send.at[side, row],
            t_recv.at[side, row], side_device(side),
        )

    def m_copy(group, src, dst):
        return remote(
            part_ref.at[group], mean_ref.at[group, src],
            m_send.at[group, dst], m_recv.at[group, src], {"row": dst},
        )

    def g_copy(src, dst):
        return remote(
            grad_ref.at[dst], out_ref.at[:, head_lanes(src)], g_send.at[dst], g_recv.at[src],
            {"pipe": pipe - 1, "row": dst},
        )

    def work():
        loop(1, HEADS, lambda hop: greet({"row": to(hop)}))
        both(lambda side: greet(side_device(side)))
        local = [
            pltpu.make_async_copy(x_far.at[:, head_lanes(me)], x3_ref.at[1, me], local_sem.at[0]),
            pltpu.make_async_copy(cot_far.at[:, head_lanes(me)], cot_ref.at[me], local_sem.at[1]),
            pltpu.make_async_copy(gains_far.at[:, :, head_lanes(me)], gains_ref, local_sem.at[2]),
        ]
        for copy in local:
            copy.start()
        x_float = x_ref[...].astype(F32)
        square = jnp.mean(x_float * x_float, axis=-1, keepdims=True)
        inverse = jnp.broadcast_to(lax.rsqrt(square + EPSILON), (area, area))
        inv_ref[...] = inverse.T[:1]

        key = lax.broadcasted_iota(jnp.int32, (wide, area), 0)
        query = lax.broadcasted_iota(jnp.int32, (wide, area), 1)
        key_tile = 2 * (key // area) + (key // TILE) % 2
        query_tile = (query // TILE) % 2
        near = (key_tile >= query_tile) & (key_tile <= query_tile + 2 * REACH)
        inside = (col * 2 + key_tile >= REACH) & (col * 2 + key_tile < 2 * cols + REACH)
        bias_ref[0] = jnp.full((wide, area), NEGATIVE, F32)
        bias_ref[1] = jnp.where(near & inside, 0.0, NEGATIVE)
        for pad in (0, 1, rows + 2, rows + 3):
            kv_ref[pad] = jnp.zeros((wide, 2 * depth), BF16)
            kt_ref[pad] = jnp.zeros((depth, wide), BF16)
            qd_ref[pad] = jnp.zeros((2 * area, 2 * depth), BF16)
        for key_line, slot in ((0, 0), (0, 1), (1, 0), (rows - 2, 4), (rows - 1, 3), (rows - 1, 4)):
            w_ref[key_line + REACH, :, slot * 2 * area : (slot + 1) * 2 * area] = jnp.zeros(
                (wide, 2 * area), BF16
            )
        pl.semaphore_wait(
            barrier, 2 * HEADS - 1 + has_left.astype(jnp.int32) + has_right.astype(jnp.int32)
        )

        loop(1, HEADS, lambda hop: r_copy(me, to(hop)).start())
        loop(1, HEADS, lambda hop: x_copy(me, to(hop)).start())
        own_r = pltpu.make_async_copy(inv_ref, r3_ref.at[1, me], local_sem.at[3])
        own_r.start()
        loop(1, HEADS, lambda hop: c_copy(me, to(hop)).start())
        for copy in local:
            copy.wait()
        own_r.wait()

        gn = gains_ref[0]
        gq = gains_ref[1] * (1.0 / math.sqrt(HEAD_DIM))
        gk = gains_ref[2]
        gv = gains_ref[3]
        go = gains_ref[4]

        def prepare(row, block):
            inverse = jnp.broadcast_to(r3_ref[block, row], (area, area)).T
            x_float = x3_ref[block, row].astype(F32)
            normed = (x_float * inverse * gn).astype(BF16).astype(F32)
            keys = (normed * gk).astype(BF16)
            lanes = slice(block * area, (block + 1) * area)
            kv_ref[row + REACH, lanes, :depth] = keys
            kv_ref[row + REACH, lanes, depth:] = (normed * gv).astype(BF16)
            kt_ref[row + REACH, :, lanes] = keys.T
            if block == 1:
                qd_ref[row + REACH, :area, :depth] = (normed * gq).astype(BF16)
                qd_ref[row + REACH, :area, depth:] = jnp.zeros((area, depth), BF16)
                qd_ref[row + REACH, area:, :depth] = jnp.zeros((area, depth), BF16)

        def pass_on(src):
            both(lambda side: fx_copy(src, side).start())
            both(lambda side: fr_copy(src, side).start())
            prepare(src, 1)

        pass_on(me)

        def arrive(hop):
            src = back(hop)
            x_copy(src, me).wait_recv()
            r_copy(src, me).wait_recv()
            pass_on(src)

        loop(1, HEADS, arrive)

        def await_beside(src, side):
            fx_copy(src, side).wait_recv()
            fr_copy(src, side).wait_recv()

        def blank(src, block):
            lanes = slice(block * area, (block + 1) * area)
            kv_ref[src + REACH, lanes, :] = jnp.zeros((area, 2 * depth), BF16)
            kt_ref[src + REACH, :, lanes] = jnp.zeros((depth, area), BF16)

        def beside(pair):
            sources = (back(2 * pair), back(2 * pair + 1))

            @pl.when(jnp.logical_and(has_left, has_right))
            def _():
                for src in sources:
                    await_beside(src, 0)
                    await_beside(src, 1)
                for src in sources:
                    prepare(src, 0)
                    prepare(src, 2)

            @pl.when(jnp.logical_not(has_left))
            def _():
                for src in sources:
                    await_beside(src, 0)
                for src in sources:
                    prepare(src, 2)
                    blank(src, 0)

            @pl.when(jnp.logical_not(has_right))
            def _():
                for src in sources:
                    await_beside(src, 1)
                for src in sources:
                    prepare(src, 0)
                    blank(src, 2)

        loop(0, HEADS // 2, beside)

        def lines_of(block):
            return slice(block * area, (block + 1) * area)

        def soften(row):
            queries = qd_ref[row + REACH, :area, :depth]
            tops = []
            totals = []
            for off in range(SPAN):
                far = row + off - REACH
                valid = jnp.logical_and(far >= 0, far < rows)
                index = valid.astype(jnp.int32)
                for block in range(3):
                    lines = lines_of(block)
                    scores = dot(kv_ref[row + off, lines, :depth], queries, ((1,), (1,)))
                    if block == 1:
                        scores = scores + jnp.where(valid, 0.0, NEGATIVE)
                    else:
                        scores = scores + bias_ref[index, lines, :]
                    top = jnp.max(fold(scores, jnp.max), axis=0, keepdims=True)
                    raised = jnp.exp(scores - top)
                    p_ref[row, off, lines, :] = raised
                    tops.append(top)
                    totals.append(fold(raised, jnp.sum))
            peak = functools.reduce(jnp.maximum, tops)
            shares = [jnp.exp(top - peak) for top in tops]
            total = jnp.sum(sum(t * f for t, f in zip(totals, shares)), axis=0, keepdims=True)
            inverse = 1.0 / total
            for index, share in enumerate(shares):
                scale_ref[row, index : index + 1, :] = share * inverse

        loop(0, rows, soften)

        def upstream(hop):
            src = back(hop)

            @pl.when(hop > 0)
            def _():
                c_copy(src, me).wait_recv()

            qd_ref[src + REACH, area:, depth:] = (cot_ref[src].astype(F32) * go).astype(BF16)

        loop(0, HEADS, upstream)

        def grade(row, buffer):
            grads = qd_ref[row + REACH, area:, depth:]
            delta = jnp.zeros((8, area), F32)
            for off in range(SPAN):
                slot = 2 * area * (SPAN - 1 - off)
                for block in range(3):
                    lines = lines_of(block)
                    index = 3 * off + block
                    product = dot(kv_ref[row + off, lines, depth:], grads, ((1,), (1,)))
                    dp_ref[buffer, off, lines, :] = product
                    weights = p_ref[row, off, lines, :] * scale_ref[row, index : index + 1, :]
                    rounded = weights.astype(BF16)
                    w_ref[row + off, lines, slot + area : slot + 2 * area] = rounded
                    delta = delta + fold(rounded.astype(F32) * product, jnp.sum)
            delta_ref[row] = jnp.sum(delta, axis=0, keepdims=True)

        def score(row, buffer):
            delta = delta_ref[row]
            turned = jnp.zeros((depth, area), F32)
            for off in range(SPAN):
                slot = 2 * area * (SPAN - 1 - off)
                pieces = []
                for block in range(3):
                    lines = lines_of(block)
                    index = 3 * off + block
                    weights = p_ref[row, off, lines, :] * scale_ref[row, index : index + 1, :]
                    dscore = (weights * (dp_ref[buffer, off, lines, :] - delta)).astype(BF16)
                    w_ref[row + off, lines, slot : slot + area] = dscore
                    pieces.append(dscore)
                dscore = jnp.concatenate(pieces, axis=0)
                turned = turned + dot(kt_ref[row + off], dscore, ((1,), (0,)))
            own_ref[row] = turned.T * gq

        def key_line(row):
            pairs = qd_ref[pl.ds(row, SPAN)].reshape(SPAN * 2 * area, 2 * depth)
            grads = dot(w_ref[row + REACH], pairs, ((1,), (0,)))
            terms = grads[:, :depth] * gk + grads[:, depth:] * gv
            term_ref[0, row] = terms[:area]
            own_ref[row] = own_ref[row] + terms[area : 2 * area]
            term_ref[1, row] = terms[2 * area :]

        def collect(row):
            both(lambda side: t_copy(row, 1 - side).wait_recv())
            dnormed = own_ref[row]
            dnormed = dnormed + jnp.where(has_right, from_ref[0, row], 0.0)
            dnormed = dnormed + jnp.where(has_left, from_ref[1, row], 0.0)
            scaled = dnormed * gn
            own_ref[row] = scaled
            product = (x3_ref[1, row].astype(F32) * scaled).T
            part_ref[row // GROUP, pl.ds(row % GROUP, 1), :] = jnp.sum(
                product, axis=0, keepdims=True
            )

        def own_part(group):
            return pltpu.make_async_copy(
                part_ref.at[group], mean_ref.at[group, me], m_local.at[group]
            )

        def share(row):
            @pl.when(row % GROUP == GROUP - 1)
            def _():
                group = row // GROUP
                own_part(group).start()
                loop(1, HEADS, lambda hop: m_copy(group, me, to(hop)).start())

        def close(row):
            @pl.when(row % GROUP == GROUP - 1)
            def _():
                group = row // GROUP
                own_part(group).wait()
                loop(1, HEADS, lambda hop: m_copy(group, back(hop), me).wait_recv())
                means = jnp.sum(mean_ref[group], axis=0) / (rows * depth)
                for line in range(GROUP):
                    each = group * GROUP + line
                    inverse = jnp.broadcast_to(r3_ref[1, each], (area, area))
                    pull = (inverse * inverse * inverse * means[line : line + 1]).T
                    grad = (
                        cot_ref[each].astype(F32)
                        + inverse.T * own_ref[each]
                        - x3_ref[1, each].astype(F32) * pull
                    )
                    grad_ref[each] = grad.astype(BF16)

        def give_back(row):
            @pl.when(row % GROUP == GROUP - 1)
            def _():
                for line in range(GROUP):
                    g_copy(me, row - line).start()

        def send_terms(row):
            both(lambda side: t_copy(row, side).start())

        def pair(turn):
            first = 2 * turn

            @pl.when(jnp.logical_and(turn >= 3, first < rows))
            def _():
                key_line(first - 5)
                key_line(first - 4)
                score(first - 1, 1)
                grade(first, 0)
                score(first, 0)
                grade(first + 1, 1)

            @pl.when(turn < 3)
            def _():
                @pl.when(turn == 2)
                def _():
                    key_line(first - 4)

                @pl.when(turn > 0)
                def _():
                    score(first - 1, 1)

                grade(first, 0)
                score(first, 0)
                grade(first + 1, 1)

            @pl.when(first == rows)
            def _():
                key_line(first - 5)
                key_line(first - 4)
                score(first - 1, 1)

            @pl.when(first == rows + 2)
            def _():
                for line in (-5, -4, -3):
                    key_line(first + line)

            for part in range(2):
                for act, lag in (
                    (send_terms, 6),
                    (collect, 6 + TERMS_LAG),
                    (share, 7 + TERMS_LAG),
                    (close, 7 + TERMS_LAG + MEAN_LAG),
                    (give_back, 8 + TERMS_LAG + MEAN_LAG),
                ):
                    row = first + part - lag

                    @pl.when(jnp.logical_and(row >= 0, row < rows))
                    def _():
                        act(row)

        loop(0, (rows + 8 + TERMS_LAG + MEAN_LAG + 1) // 2, pair)

    @pl.when(pipe < pipes - 1)
    def _():
        loop(0, rows, lambda row: greet({"pipe": pipe + 1, "row": row}))

    @pl.when(pipe == pipes - 1)
    def _():
        out_ref[...] = jnp.zeros_like(out_ref)

    @pl.when(pipe > 0)
    def _():
        work()

    @pl.when(pipe < pipes - 1)
    def _():
        def wait_grad(row):
            remote(
                grad_ref.at[0], out_ref.at[:, head_lanes(row)], g_send.at[0], g_recv.at[row],
                {"pipe": pipe + 1, "row": row},
            ).wait_recv()

        loop(0, rows, wait_grad)

    @pl.when(pipe > 0)
    def _():
        def drain(hop):
            x_copy(me, to(hop)).wait_send()
            r_copy(me, to(hop)).wait_send()
            c_copy(me, to(hop)).wait_send()

        loop(1, HEADS, drain)

        def drain_row(row):
            both(lambda side: fx_copy(row, side).wait_send())
            both(lambda side: fr_copy(row, side).wait_send())
            both(lambda side: t_copy(row, side).wait_send())
            g_copy(me, row).wait_send()

        loop(0, rows, drain_row)

        def drain_group(group):
            loop(1, HEADS, lambda hop: m_copy(group, me, to(hop)).wait_send())

        loop(0, rows // GROUP, drain_group)


def per_device(saved_in, cotangent, section_gains):
    _, tall, across, width = saved_in.shape
    area = tall * across
    rows = HEADS
    wide = 3 * area
    x = saved_in.reshape(area, width)
    cot = cotangent.reshape(area, width)
    gains = section_gains.transpose(1, 0, 2)
    far = pl.BlockSpec(memory_space=pl.ANY)
    vmem = pl.BlockSpec(memory_space=pltpu.VMEM)
    dma = pltpu.SemaphoreType.DMA
    grad = pl.pallas_call(
        section_kernel,
        out_shape=jax.ShapeDtypeStruct((area, width), BF16),
        in_specs=[vmem, far, far, far],
        out_specs=vmem,
        scratch_shapes=[
            pltpu.VMEM((3, rows, area, HEAD_DIM), BF16),
            pltpu.VMEM((3, rows, 1, area), F32),
            pltpu.VMEM((rows, area, HEAD_DIM), BF16),
            pltpu.VMEM((gains.shape[0], 1, HEAD_DIM), F32),
            pltpu.VMEM((1, area), F32),
            pltpu.VMEM((2, wide, area), F32),
            pltpu.VMEM((rows + 4, wide, 2 * HEAD_DIM), BF16),
            pltpu.VMEM((rows + 4, HEAD_DIM, wide), BF16),
            pltpu.VMEM((rows + 4, 2 * area, 2 * HEAD_DIM), BF16),
            pltpu.VMEM((rows + 4, wide, SPAN * 2 * area), BF16),
            pltpu.VMEM((rows, SPAN, wide, area), F32),
            pltpu.VMEM((rows, 3 * SPAN, area), F32),
            pltpu.VMEM((rows, 1, area), F32),
            pltpu.VMEM((2, SPAN, wide, area), F32),
            pltpu.VMEM((rows, area, HEAD_DIM), F32),
            pltpu.VMEM((2, rows, area, HEAD_DIM), F32),
            pltpu.VMEM((2, rows, area, HEAD_DIM), F32),
            pltpu.VMEM((rows // GROUP, GROUP, area), F32),
            pltpu.VMEM((rows // GROUP, HEADS, GROUP, area), F32),
            pltpu.VMEM((rows, area, HEAD_DIM), BF16),
            dma((4,)),
            dma((HEADS,)), dma((HEADS,)), dma((HEADS,)), dma((HEADS,)), dma((HEADS,)), dma((HEADS,)),
            dma((2, HEADS)), dma((2, HEADS)), dma((2, HEADS)), dma((2, HEADS)),
            dma((2, rows)), dma((2, rows)),
            dma((rows // GROUP,)), dma((rows // GROUP, HEADS)), dma((rows // GROUP, HEADS)),
            dma((rows,)), dma((HEADS,)),
        ],
        compiler_params=pltpu.CompilerParams(
            collective_id=0, has_side_effects=True, vmem_limit_bytes=60 * 1024 * 1024
        ),
        name="section_backward",
    )(x, x, cot, gains)
    return grad.reshape(1, tall, across, width)


def solution(mesh):
    return jax.shard_map(
        per_device,
        mesh=mesh,
        in_specs=(
            P("pipe", "row", "col", None),
            P("pipe", "row", "col", None),
            P("pipe", None, None),
        ),
        out_specs=P("pipe", "row", "col", None),
        check_vma=False,
    )
```

```python
import functools
import math

import jax
import jax.numpy as jnp
from jax import lax
from jax.experimental import pallas as pl
from jax.experimental.pallas import tpu as pltpu
from jax.sharding import PartitionSpec as P

HEADS = 16
HEAD_DIM = 128
TILE = 8
SPAN = 5
REACH = SPAN // 2
GROUP = 4
TERMS_LAG = 4
MEAN_LAG = 12

NEGATIVE = -1e30
EPSILON = 1e-06
F32 = jnp.float32
BF16 = jnp.bfloat16
MESH = pl.DeviceIdType.MESH


def dot(left, right, dims):
    return lax.dot_general(left, right, (dims, ((), ())), preferred_element_type=F32)


def fold(block, op):
    rows, lanes = block.shape
    return op(block.reshape(rows // 8, 8, lanes), axis=0)


def head_lanes(head):
    return pl.ds(pl.multiple_of(head * HEAD_DIM, HEAD_DIM), HEAD_DIM)


def remote(src, dst, send, recv, device):
    return pltpu.make_async_remote_copy(
        src_ref=src, dst_ref=dst, send_sem=send, recv_sem=recv,
        device_id=device, device_id_type=MESH,
    )


def loop(low, high, step):
    def body(index, carry):
        step(index)
        return carry

    lax.fori_loop(low, high, body, 0)


def section_kernel(
    x_ref, x_far, cot_far, gains_far, out_ref,
    x3_ref, r3_ref, cot_ref, gains_ref, inv_ref, bias_ref, kv_ref, kt_ref, qd_ref, w_ref,
    p_ref, scale_ref, delta_ref, dp_ref, own_ref, term_ref, from_ref, part_ref, mean_ref, grad_ref,
    local_sem, x_send, x_recv, r_send, r_recv, c_send, c_recv,
    fx_send, fx_recv, fr_send, fr_recv, t_send, t_recv, m_local, m_send, m_recv, g_send, g_recv,
):
    area = x_ref.shape[0]
    rows = HEADS
    depth = HEAD_DIM
    wide = 3 * area
    me = lax.axis_index("row")
    col = lax.axis_index("col")
    cols = lax.axis_size("col")
    pipe = lax.axis_index("pipe")
    pipes = lax.axis_size("pipe")
    has_left = col > 0
    has_right = col < cols - 1
    barrier = pltpu.get_barrier_semaphore()

    def greet(device):
        pl.semaphore_signal(barrier, inc=1, device_id=device, device_id_type=MESH)

    def to(hop):
        return lax.rem(me + hop, HEADS)

    def back(hop):
        return lax.rem(me + HEADS - hop, HEADS)

    def both(act):
        @pl.when(has_left)
        def _():
            act(0)

        @pl.when(has_right)
        def _():
            act(1)

    def side_device(side):
        return {"col": col - 1} if side == 0 else {"col": col + 1}

    def x_copy(src, dst):
        return remote(
            x_far.at[:, head_lanes(dst)], x3_ref.at[1, src], x_send.at[dst], x_recv.at[src],
            {"row": dst},
        )

    def r_copy(src, dst):
        return remote(inv_ref, r3_ref.at[1, src], r_send.at[dst], r_recv.at[src], {"row": dst})

    def c_copy(src, dst):
        return remote(
            cot_far.at[:, head_lanes(dst)], cot_ref.at[src], c_send.at[dst], c_recv.at[src],
            {"row": dst},
        )

    def fx_copy(src, side):
        return remote(
            x3_ref.at[1, src], x3_ref.at[2 - 2 * side, src], fx_send.at[side, src],
            fx_recv.at[side, src], side_device(side),
        )

    def fr_copy(src, side):
        return remote(
            r3_ref.at[1, src], r3_ref.at[2 - 2 * side, src], fr_send.at[side, src],
            fr_recv.at[side, src], side_device(side),
        )

    def t_copy(row, side):
        return remote(
            term_ref.at[side, row], from_ref.at[side, row], t_send.at[side, row],
            t_recv.at[side, row], side_device(side),
        )

    def m_copy(group, src, dst):
        return remote(
            part_ref.at[group], mean_ref.at[group, src],
            m_send.at[group, dst], m_recv.at[group, src], {"row": dst},
        )

    def g_copy(src, dst):
        return remote(
            grad_ref.at[dst], out_ref.at[:, head_lanes(src)], g_send.at[dst], g_recv.at[src],
            {"pipe": pipe - 1, "row": dst},
        )

    def work():
        loop(1, HEADS, lambda hop: greet({"row": to(hop)}))
        both(lambda side: greet(side_device(side)))
        local = [
            pltpu.make_async_copy(x_far.at[:, head_lanes(me)], x3_ref.at[1, me], local_sem.at[0]),
            pltpu.make_async_copy(cot_far.at[:, head_lanes(me)], cot_ref.at[me], local_sem.at[1]),
            pltpu.make_async_copy(gains_far.at[:, :, head_lanes(me)], gains_ref, local_sem.at[2]),
        ]
        for copy in local:
            copy.start()
        x_float = x_ref[...].astype(F32)
        square = jnp.mean(x_float * x_float, axis=-1, keepdims=True)
        inverse = jnp.broadcast_to(lax.rsqrt(square + EPSILON), (area, area))
        inv_ref[...] = inverse.T[:1]

        key = lax.broadcasted_iota(jnp.int32, (wide, area), 0)
        query = lax.broadcasted_iota(jnp.int32, (wide, area), 1)
        key_tile = 2 * (key // area) + (key // TILE) % 2
        query_tile = (query // TILE) % 2
        near = (key_tile >= query_tile) & (key_tile <= query_tile + 2 * REACH)
        inside = (col * 2 + key_tile >= REACH) & (col * 2 + key_tile < 2 * cols + REACH)
        bias_ref[0] = jnp.full((wide, area), NEGATIVE, F32)
        bias_ref[1] = jnp.where(near & inside, 0.0, NEGATIVE)
        for pad in (0, 1, rows + 2, rows + 3):
            kv_ref[pad] = jnp.zeros((wide, 2 * depth), BF16)
            kt_ref[pad] = jnp.zeros((depth, wide), BF16)
            qd_ref[pad] = jnp.zeros((2 * area, 2 * depth), BF16)
        for key_line, slot in ((0, 0), (0, 1), (1, 0), (rows - 2, 4), (rows - 1, 3), (rows - 1, 4)):
            w_ref[key_line + REACH, :, slot * 2 * area : (slot + 1) * 2 * area] = jnp.zeros(
                (wide, 2 * area), BF16
            )
        pl.semaphore_wait(
            barrier, 2 * HEADS - 1 + has_left.astype(jnp.int32) + has_right.astype(jnp.int32)
        )

        loop(1, HEADS, lambda hop: r_copy(me, to(hop)).start())
        loop(1, HEADS, lambda hop: x_copy(me, to(hop)).start())
        own_r = pltpu.make_async_copy(inv_ref, r3_ref.at[1, me], local_sem.at[3])
        own_r.start()
        loop(1, HEADS, lambda hop: c_copy(me, to(hop)).start())
        for copy in local:
            copy.wait()
        own_r.wait()

        gn = gains_ref[0]
        gq = gains_ref[1] * (1.0 / math.sqrt(HEAD_DIM))
        gk = gains_ref[2]
        gv = gains_ref[3]
        go = gains_ref[4]

        def prepare(row, block):
            inverse = jnp.broadcast_to(r3_ref[block, row], (area, area)).T
            x_float = x3_ref[block, row].astype(F32)
            normed = (x_float * inverse * gn).astype(BF16).astype(F32)
            keys = (normed * gk).astype(BF16)
            lanes = slice(block * area, (block + 1) * area)
            kv_ref[row + REACH, lanes, :depth] = keys
            kv_ref[row + REACH, lanes, depth:] = (normed * gv).astype(BF16)
            kt_ref[row + REACH, :, lanes] = keys.T
            if block == 1:
                qd_ref[row + REACH, :area, :depth] = (normed * gq).astype(BF16)
                qd_ref[row + REACH, :area, depth:] = jnp.zeros((area, depth), BF16)
                qd_ref[row + REACH, area:, :depth] = jnp.zeros((area, depth), BF16)

        def pass_on(src):
            both(lambda side: fx_copy(src, side).start())
            both(lambda side: fr_copy(src, side).start())
            prepare(src, 1)

        pass_on(me)

        def arrive(hop):
            src = back(hop)
            x_copy(src, me).wait_recv()
            r_copy(src, me).wait_recv()
            pass_on(src)

        loop(1, HEADS, arrive)

        def await_beside(src, side):
            fx_copy(src, side).wait_recv()
            fr_copy(src, side).wait_recv()

        def blank(src, block):
            lanes = slice(block * area, (block + 1) * area)
            kv_ref[src + REACH, lanes, :] = jnp.zeros((area, 2 * depth), BF16)
            kt_ref[src + REACH, :, lanes] = jnp.zeros((depth, area), BF16)

        def beside(pair):
            sources = (back(2 * pair), back(2 * pair + 1))

            @pl.when(jnp.logical_and(has_left, has_right))
            def _():
                for src in sources:
                    await_beside(src, 0)
                    await_beside(src, 1)
                for src in sources:
                    prepare(src, 0)
                    prepare(src, 2)

            @pl.when(jnp.logical_not(has_left))
            def _():
                for src in sources:
                    await_beside(src, 0)
                for src in sources:
                    prepare(src, 2)
                    blank(src, 0)

            @pl.when(jnp.logical_not(has_right))
            def _():
                for src in sources:
                    await_beside(src, 1)
                for src in sources:
                    prepare(src, 0)
                    blank(src, 2)

        loop(0, HEADS // 2, beside)

        def lines_of(block):
            return slice(block * area, (block + 1) * area)

        def soften(row):
            queries = qd_ref[row + REACH, :area, :depth]
            tops = []
            totals = []
            for off in range(SPAN):
                far = row + off - REACH
                valid = jnp.logical_and(far >= 0, far < rows)
                index = valid.astype(jnp.int32)
                for block in range(3):
                    lines = lines_of(block)
                    scores = dot(kv_ref[row + off, lines, :depth], queries, ((1,), (1,)))
                    if block == 1:
                        scores = scores + jnp.where(valid, 0.0, NEGATIVE)
                    else:
                        scores = scores + bias_ref[index, lines, :]
                    top = jnp.max(fold(scores, jnp.max), axis=0, keepdims=True)
                    raised = jnp.exp(scores - top)
                    p_ref[row, off, lines, :] = raised
                    tops.append(top)
                    totals.append(fold(raised, jnp.sum))
            peak = functools.reduce(jnp.maximum, tops)
            shares = [jnp.exp(top - peak) for top in tops]
            total = jnp.sum(sum(t * f for t, f in zip(totals, shares)), axis=0, keepdims=True)
            inverse = 1.0 / total
            for index, share in enumerate(shares):
                scale_ref[row, index : index + 1, :] = share * inverse

        loop(0, rows, soften)

        def upstream(hop):
            src = back(hop)

            @pl.when(hop > 0)
            def _():
                c_copy(src, me).wait_recv()

            qd_ref[src + REACH, area:, depth:] = (cot_ref[src].astype(F32) * go).astype(BF16)

        loop(0, HEADS, upstream)

        def grade(row, buffer):
            grads = qd_ref[row + REACH, area:, depth:]
            delta = jnp.zeros((8, area), F32)
            for off in range(SPAN):
                slot = 2 * area * (SPAN - 1 - off)
                for block in range(3):
                    lines = lines_of(block)
                    index = 3 * off + block
                    product = dot(kv_ref[row + off, lines, depth:], grads, ((1,), (1,)))
                    dp_ref[buffer, off, lines, :] = product
                    weights = p_ref[row, off, lines, :] * scale_ref[row, index : index + 1, :]
                    rounded = weights.astype(BF16)
                    w_ref[row + off, lines, slot + area : slot + 2 * area] = rounded
                    delta = delta + fold(rounded.astype(F32) * product, jnp.sum)
            delta_ref[row] = jnp.sum(delta, axis=0, keepdims=True)

        def score(row, buffer):
            delta = delta_ref[row]
            turned = jnp.zeros((depth, area), F32)
            for off in range(SPAN):
                slot = 2 * area * (SPAN - 1 - off)
                pieces = []
                for block in range(3):
                    lines = lines_of(block)
                    index = 3 * off + block
                    weights = p_ref[row, off, lines, :] * scale_ref[row, index : index + 1, :]
                    dscore = (weights * (dp_ref[buffer, off, lines, :] - delta)).astype(BF16)
                    w_ref[row + off, lines, slot : slot + area] = dscore
                    pieces.append(dscore)
                dscore = jnp.concatenate(pieces, axis=0)
                turned = turned + dot(kt_ref[row + off], dscore, ((1,), (0,)))
            own_ref[row] = turned.T * gq

        def key_line(row):
            pairs = qd_ref[pl.ds(row, SPAN)].reshape(SPAN * 2 * area, 2 * depth)
            grads = dot(w_ref[row + REACH], pairs, ((1,), (0,)))
            terms = grads[:, :depth] * gk + grads[:, depth:] * gv
            term_ref[0, row] = terms[:area]
            own_ref[row] = own_ref[row] + terms[area : 2 * area]
            term_ref[1, row] = terms[2 * area :]

        def collect(row):
            both(lambda side: t_copy(row, 1 - side).wait_recv())
            dnormed = own_ref[row]
            dnormed = dnormed + jnp.where(has_right, from_ref[0, row], 0.0)
            dnormed = dnormed + jnp.where(has_left, from_ref[1, row], 0.0)
            scaled = dnormed * gn
            own_ref[row] = scaled
            product = (x3_ref[1, row].astype(F32) * scaled).T
            part_ref[row // GROUP, pl.ds(row % GROUP, 1), :] = jnp.sum(
                product, axis=0, keepdims=True
            )

        def own_part(group):
            return pltpu.make_async_copy(
                part_ref.at[group], mean_ref.at[group, me], m_local.at[group]
            )

        def share(row):
            @pl.when(row % GROUP == GROUP - 1)
            def _():
                group = row // GROUP
                own_part(group).start()
                loop(1, HEADS, lambda hop: m_copy(group, me, to(hop)).start())

        def close(row):
            @pl.when(row % GROUP == GROUP - 1)
            def _():
                group = row // GROUP
                own_part(group).wait()
                loop(1, HEADS, lambda hop: m_copy(group, back(hop), me).wait_recv())
                means = jnp.sum(mean_ref[group], axis=0) / (rows * depth)
                for line in range(GROUP):
                    each = group * GROUP + line
                    inverse = jnp.broadcast_to(r3_ref[1, each], (area, area))
                    pull = (inverse * inverse * inverse * means[line : line + 1]).T
                    grad = (
                        cot_ref[each].astype(F32)
                        + inverse.T * own_ref[each]
                        - x3_ref[1, each].astype(F32) * pull
                    )
                    grad_ref[each] = grad.astype(BF16)

        def give_back(row):
            @pl.when(row % GROUP == GROUP - 1)
            def _():
                for line in range(GROUP):
                    g_copy(me, row - line).start()

        def send_terms(row):
            both(lambda side: t_copy(row, side).start())

        def pair(turn):
            first = 2 * turn

            @pl.when(jnp.logical_and(turn >= 3, first < rows))
            def _():
                key_line(first - 5)
                key_line(first - 4)
                score(first - 1, 1)
                grade(first, 0)
                score(first, 0)
                grade(first + 1, 1)

            @pl.when(turn < 3)
            def _():
                @pl.when(turn == 2)
                def _():
                    key_line(first - 4)

                @pl.when(turn > 0)
                def _():
                    score(first - 1, 1)

                grade(first, 0)
                score(first, 0)
                grade(first + 1, 1)

            @pl.when(first == rows)
            def _():
                key_line(first - 5)
                key_line(first - 4)
                score(first - 1, 1)

            @pl.when(first == rows + 2)
            def _():
                for line in (-5, -4, -3):
                    key_line(first + line)

            for part in range(2):
                for act, lag in (
                    (send_terms, 6),
                    (collect, 6 + TERMS_LAG),
                    (share, 7 + TERMS_LAG),
                    (close, 7 + TERMS_LAG + MEAN_LAG),
                    (give_back, 8 + TERMS_LAG + MEAN_LAG),
                ):
                    row = first + part - lag

                    @pl.when(jnp.logical_and(row >= 0, row < rows))
                    def _():
                        act(row)

        loop(0, (rows + 8 + TERMS_LAG + MEAN_LAG + 1) // 2, pair)

    @pl.when(pipe < pipes - 1)
    def _():
        loop(0, rows, lambda row: greet({"pipe": pipe + 1, "row": row}))

    @pl.when(pipe == pipes - 1)
    def _():
        out_ref[...] = jnp.zeros_like(out_ref)

    @pl.when(pipe > 0)
    def _():
        work()

    @pl.when(pipe < pipes - 1)
    def _():
        def wait_grad(row):
            remote(
                grad_ref.at[0], out_ref.at[:, head_lanes(row)], g_send.at[0], g_recv.at[row],
                {"pipe": pipe + 1, "row": row},
            ).wait_recv()

        loop(0, rows, wait_grad)

    @pl.when(pipe > 0)
    def _():
        def drain(hop):
            x_copy(me, to(hop)).wait_send()
            r_copy(me, to(hop)).wait_send()
            c_copy(me, to(hop)).wait_send()

        loop(1, HEADS, drain)

        def drain_row(row):
            both(lambda side: fx_copy(row, side).wait_send())
            both(lambda side: fr_copy(row, side).wait_send())
            both(lambda side: t_copy(row, side).wait_send())
            g_copy(me, row).wait_send()

        loop(0, rows, drain_row)

        def drain_group(group):
            loop(1, HEADS, lambda hop: m_copy(group, me, to(hop)).wait_send())

        loop(0, rows // GROUP, drain_group)


def per_device(saved_in, cotangent, section_gains):
    _, tall, across, width = saved_in.shape
    area = tall * across
    rows = HEADS
    wide = 3 * area
    x = saved_in.reshape(area, width)
    cot = cotangent.reshape(area, width)
    gains = section_gains.transpose(1, 0, 2)
    far = pl.BlockSpec(memory_space=pl.ANY)
    vmem = pl.BlockSpec(memory_space=pltpu.VMEM)
    dma = pltpu.SemaphoreType.DMA
    grad = pl.pallas_call(
        section_kernel,
        out_shape=jax.ShapeDtypeStruct((area, width), BF16),
        in_specs=[vmem, far, far, far],
        out_specs=vmem,
        scratch_shapes=[
            pltpu.VMEM((3, rows, area, HEAD_DIM), BF16),
            pltpu.VMEM((3, rows, 1, area), F32),
            pltpu.VMEM((rows, area, HEAD_DIM), BF16),
            pltpu.VMEM((gains.shape[0], 1, HEAD_DIM), F32),
            pltpu.VMEM((1, area), F32),
            pltpu.VMEM((2, wide, area), F32),
            pltpu.VMEM((rows + 4, wide, 2 * HEAD_DIM), BF16),
            pltpu.VMEM((rows + 4, HEAD_DIM, wide), BF16),
            pltpu.VMEM((rows + 4, 2 * area, 2 * HEAD_DIM), BF16),
            pltpu.VMEM((rows + 4, wide, SPAN * 2 * area), BF16),
            pltpu.VMEM((rows, SPAN, wide, area), F32),
            pltpu.VMEM((rows, 3 * SPAN, area), F32),
            pltpu.VMEM((rows, 1, area), F32),
            pltpu.VMEM((2, SPAN, wide, area), F32),
            pltpu.VMEM((rows, area, HEAD_DIM), F32),
            pltpu.VMEM((2, rows, area, HEAD_DIM), F32),
            pltpu.VMEM((2, rows, area, HEAD_DIM), F32),
            pltpu.VMEM((rows // GROUP, GROUP, area), F32),
            pltpu.VMEM((rows // GROUP, HEADS, GROUP, area), F32),
            pltpu.VMEM((rows, area, HEAD_DIM), BF16),
            dma((4,)),
            dma((HEADS,)), dma((HEADS,)), dma((HEADS,)), dma((HEADS,)), dma((HEADS,)), dma((HEADS,)),
            dma((2, HEADS)), dma((2, HEADS)), dma((2, HEADS)), dma((2, HEADS)),
            dma((2, rows)), dma((2, rows)),
            dma((rows // GROUP,)), dma((rows // GROUP, HEADS)), dma((rows // GROUP, HEADS)),
            dma((rows,)), dma((HEADS,)),
        ],
        compiler_params=pltpu.CompilerParams(
            collective_id=0, has_side_effects=True, vmem_limit_bytes=60 * 1024 * 1024
        ),
        name="section_backward",
    )(x, x, cot, gains)
    return grad.reshape(1, tall, across, width)


def solution(mesh):
    return jax.shard_map(
        per_device,
        mesh=mesh,
        in_specs=(
            P("pipe", "row", "col", None),
            P("pipe", "row", "col", None),
            P("pipe", None, None),
        ),
        out_specs=P("pipe", "row", "col", None),
        check_vma=False,
    )
```

```python
import functools
import math

import jax
import jax.numpy as jnp
from jax import lax
from jax.experimental import pallas as pl
from jax.experimental.pallas import tpu as pltpu
from jax.sharding import PartitionSpec as P

HEADS = 16
HEAD_DIM = 128
TILE = 8
SPAN = 5
REACH = SPAN // 2
GROUP = 4
TERMS_LAG = 4
MEAN_LAG = 12

NEGATIVE = -1e30
EPSILON = 1e-06
F32 = jnp.float32
BF16 = jnp.bfloat16
MESH = pl.DeviceIdType.MESH


def dot(left, right, dims):
    return lax.dot_general(left, right, (dims, ((), ())), preferred_element_type=F32)


def fold(block, op):
    rows, lanes = block.shape
    return op(block.reshape(rows // 8, 8, lanes), axis=0)


def head_lanes(head):
    return pl.ds(pl.multiple_of(head * HEAD_DIM, HEAD_DIM), HEAD_DIM)


def remote(src, dst, send, recv, device):
    return pltpu.make_async_remote_copy(
        src_ref=src, dst_ref=dst, send_sem=send, recv_sem=recv,
        device_id=device, device_id_type=MESH,
    )


def loop(low, high, step):
    def body(index, carry):
        step(index)
        return carry

    lax.fori_loop(low, high, body, 0)


def section_kernel(
    x_ref, x_far, cot_far, gains_far, out_ref,
    x3_ref, r3_ref, cot_ref, gains_ref, inv_ref, bias_ref, kv_ref, kt_ref, qd_ref, w_ref,
    p_ref, scale_ref, delta_ref, dp_ref, own_ref, term_ref, from_ref, part_ref, mean_ref, grad_ref,
    local_sem, x_send, x_recv, r_send, r_recv, c_send, c_recv,
    fx_send, fx_recv, fr_send, fr_recv, t_send, t_recv, m_local, m_send, m_recv, g_send, g_recv,
):
    area = x_ref.shape[0]
    rows = HEADS
    depth = HEAD_DIM
    wide = 3 * area
    me = lax.axis_index("row")
    col = lax.axis_index("col")
    cols = lax.axis_size("col")
    pipe = lax.axis_index("pipe")
    pipes = lax.axis_size("pipe")
    has_left = col > 0
    has_right = col < cols - 1
    barrier = pltpu.get_barrier_semaphore()

    def greet(device):
        pl.semaphore_signal(barrier, inc=1, device_id=device, device_id_type=MESH)

    def to(hop):
        return lax.rem(me + hop, HEADS)

    def back(hop):
        return lax.rem(me + HEADS - hop, HEADS)

    def both(act):
        @pl.when(has_left)
        def _():
            act(0)

        @pl.when(has_right)
        def _():
            act(1)

    def side_device(side):
        return {"col": col - 1} if side == 0 else {"col": col + 1}

    def x_copy(src, dst):
        return remote(
            x_far.at[:, head_lanes(dst)], x3_ref.at[1, src], x_send.at[dst], x_recv.at[src],
            {"row": dst},
        )

    def r_copy(src, dst):
        return remote(inv_ref, r3_ref.at[1, src], r_send.at[dst], r_recv.at[src], {"row": dst})

    def c_copy(src, dst):
        return remote(
            cot_far.at[:, head_lanes(dst)], cot_ref.at[src], c_send.at[dst], c_recv.at[src],
            {"row": dst},
        )

    def fx_copy(src, side):
        return remote(
            x3_ref.at[1, src], x3_ref.at[2 - 2 * side, src], fx_send.at[side, src],
            fx_recv.at[side, src], side_device(side),
        )

    def fr_copy(src, side):
        return remote(
            r3_ref.at[1, src], r3_ref.at[2 - 2 * side, src], fr_send.at[side, src],
            fr_recv.at[side, src], side_device(side),
        )

    def t_copy(row, side):
        return remote(
            term_ref.at[side, row], from_ref.at[side, row], t_send.at[side, row],
            t_recv.at[side, row], side_device(side),
        )

    def m_copy(group, src, dst):
        return remote(
            part_ref.at[group], mean_ref.at[group, src],
            m_send.at[group, dst], m_recv.at[group, src], {"row": dst},
        )

    def g_copy(src, dst):
        return remote(
            grad_ref.at[dst], out_ref.at[:, head_lanes(src)], g_send.at[dst], g_recv.at[src],
            {"pipe": pipe - 1, "row": dst},
        )

    def work():
        loop(1, HEADS, lambda hop: greet({"row": to(hop)}))
        both(lambda side: greet(side_device(side)))
        local = [
            pltpu.make_async_copy(x_far.at[:, head_lanes(me)], x3_ref.at[1, me], local_sem.at[0]),
            pltpu.make_async_copy(cot_far.at[:, head_lanes(me)], cot_ref.at[me], local_sem.at[1]),
            pltpu.make_async_copy(gains_far.at[:, :, head_lanes(me)], gains_ref, local_sem.at[2]),
        ]
        for copy in local:
            copy.start()
        x_float = x_ref[...].astype(F32)
        square = jnp.mean(x_float * x_float, axis=-1, keepdims=True)
        inverse = jnp.broadcast_to(lax.rsqrt(square + EPSILON), (area, area))
        inv_ref[...] = inverse.T[:1]

        key = lax.broadcasted_iota(jnp.int32, (wide, area), 0)
        query = lax.broadcasted_iota(jnp.int32, (wide, area), 1)
        key_tile = 2 * (key // area) + (key // TILE) % 2
        query_tile = (query // TILE) % 2
        near = (key_tile >= query_tile) & (key_tile <= query_tile + 2 * REACH)
        inside = (col * 2 + key_tile >= REACH) & (col * 2 + key_tile < 2 * cols + REACH)
        bias_ref[0] = jnp.full((wide, area), NEGATIVE, F32)
        bias_ref[1] = jnp.where(near & inside, 0.0, NEGATIVE)
        for pad in (0, 1, rows + 2, rows + 3):
            kv_ref[pad] = jnp.zeros((wide, 2 * depth), BF16)
            kt_ref[pad] = jnp.zeros((depth, wide), BF16)
            qd_ref[pad] = jnp.zeros((2 * area, 2 * depth), BF16)
        for key_line, slot in ((0, 0), (0, 1), (1, 0), (rows - 2, 4), (rows - 1, 3), (rows - 1, 4)):
            w_ref[key_line + REACH, :, slot * 2 * area : (slot + 1) * 2 * area] = jnp.zeros(
                (wide, 2 * area), BF16
            )
        pl.semaphore_wait(
            barrier, 2 * HEADS - 1 + has_left.astype(jnp.int32) + has_right.astype(jnp.int32)
        )

        loop(1, HEADS, lambda hop: r_copy(me, to(hop)).start())
        loop(1, HEADS, lambda hop: x_copy(me, to(hop)).start())
        own_r = pltpu.make_async_copy(inv_ref, r3_ref.at[1, me], local_sem.at[3])
        own_r.start()
        loop(1, HEADS, lambda hop: c_copy(me, to(hop)).start())
        for copy in local:
            copy.wait()
        own_r.wait()

        gn = gains_ref[0]
        gq = gains_ref[1] * (1.0 / math.sqrt(HEAD_DIM))
        gk = gains_ref[2]
        gv = gains_ref[3]
        go = gains_ref[4]

        def prepare(row, block):
            inverse = jnp.broadcast_to(r3_ref[block, row], (area, area)).T
            x_float = x3_ref[block, row].astype(F32)
            normed = (x_float * inverse * gn).astype(BF16).astype(F32)
            keys = (normed * gk).astype(BF16)
            lanes = slice(block * area, (block + 1) * area)
            kv_ref[row + REACH, lanes, :depth] = keys
            kv_ref[row + REACH, lanes, depth:] = (normed * gv).astype(BF16)
            kt_ref[row + REACH, :, lanes] = keys.T
            if block == 1:
                qd_ref[row + REACH, :area, :depth] = (normed * gq).astype(BF16)
                qd_ref[row + REACH, :area, depth:] = jnp.zeros((area, depth), BF16)
                qd_ref[row + REACH, area:, :depth] = jnp.zeros((area, depth), BF16)

        def pass_on(src):
            both(lambda side: fx_copy(src, side).start())
            both(lambda side: fr_copy(src, side).start())
            prepare(src, 1)

        pass_on(me)

        def arrive(hop):
            src = back(hop)
            x_copy(src, me).wait_recv()
            r_copy(src, me).wait_recv()
            pass_on(src)

        loop(1, HEADS, arrive)

        def await_beside(src, side):
            fx_copy(src, side).wait_recv()
            fr_copy(src, side).wait_recv()

        def blank(src, block):
            lanes = slice(block * area, (block + 1) * area)
            kv_ref[src + REACH, lanes, :] = jnp.zeros((area, 2 * depth), BF16)
            kt_ref[src + REACH, :, lanes] = jnp.zeros((depth, area), BF16)

        def beside(pair):
            sources = (back(2 * pair), back(2 * pair + 1))

            @pl.when(jnp.logical_and(has_left, has_right))
            def _():
                for src in sources:
                    await_beside(src, 0)
                    await_beside(src, 1)
                for src in sources:
                    prepare(src, 0)
                    prepare(src, 2)

            @pl.when(jnp.logical_not(has_left))
            def _():
                for src in sources:
                    await_beside(src, 0)
                for src in sources:
                    prepare(src, 2)
                    blank(src, 0)

            @pl.when(jnp.logical_not(has_right))
            def _():
                for src in sources:
                    await_beside(src, 1)
                for src in sources:
                    prepare(src, 0)
                    blank(src, 2)

        loop(0, HEADS // 2, beside)

        def lines_of(block):
            return slice(block * area, (block + 1) * area)

        def soften(row):
            queries = qd_ref[row + REACH, :area, :depth]
            tops = []
            totals = []
            for off in range(SPAN):
                far = row + off - REACH
                valid = jnp.logical_and(far >= 0, far < rows)
                index = valid.astype(jnp.int32)
                for block in range(3):
                    lines = lines_of(block)
                    scores = dot(kv_ref[row + off, lines, :depth], queries, ((1,), (1,)))
                    if block == 1:
                        scores = scores + jnp.where(valid, 0.0, NEGATIVE)
                    else:
                        scores = scores + bias_ref[index, lines, :]
                    top = jnp.max(fold(scores, jnp.max), axis=0, keepdims=True)
                    raised = jnp.exp(scores - top)
                    p_ref[row, off, lines, :] = raised
                    tops.append(top)
                    totals.append(fold(raised, jnp.sum))
            peak = functools.reduce(jnp.maximum, tops)
            shares = [jnp.exp(top - peak) for top in tops]
            total = jnp.sum(sum(t * f for t, f in zip(totals, shares)), axis=0, keepdims=True)
            inverse = 1.0 / total
            for index, share in enumerate(shares):
                scale_ref[row, index : index + 1, :] = share * inverse

        def soften_pair(turn):
            soften(2 * turn)
            soften(2 * turn + 1)

        loop(0, rows // 2, soften_pair)

        def upstream(hop):
            src = back(hop)

            @pl.when(hop > 0)
            def _():
                c_copy(src, me).wait_recv()

            qd_ref[src + REACH, area:, depth:] = (cot_ref[src].astype(F32) * go).astype(BF16)

        loop(0, HEADS, upstream)

        def grade(row, buffer):
            grads = qd_ref[row + REACH, area:, depth:]
            delta = jnp.zeros((8, area), F32)
            for off in range(SPAN):
                slot = 2 * area * (SPAN - 1 - off)
                for block in range(3):
                    lines = lines_of(block)
                    index = 3 * off + block
                    product = dot(kv_ref[row + off, lines, depth:], grads, ((1,), (1,)))
                    dp_ref[buffer, off, lines, :] = product
                    weights = p_ref[row, off, lines, :] * scale_ref[row, index : index + 1, :]
                    rounded = weights.astype(BF16)
                    w_ref[row + off, lines, slot + area : slot + 2 * area] = rounded
                    delta = delta + fold(rounded.astype(F32) * product, jnp.sum)
            delta_ref[row] = jnp.sum(delta, axis=0, keepdims=True)

        def score(row, buffer):
            delta = delta_ref[row]
            turned = jnp.zeros((depth, area), F32)
            for off in range(SPAN):
                slot = 2 * area * (SPAN - 1 - off)
                pieces = []
                for block in range(3):
                    lines = lines_of(block)
                    index = 3 * off + block
                    weights = p_ref[row, off, lines, :] * scale_ref[row, index : index + 1, :]
                    dscore = (weights * (dp_ref[buffer, off, lines, :] - delta)).astype(BF16)
                    w_ref[row + off, lines, slot : slot + area] = dscore
                    pieces.append(dscore)
                dscore = jnp.concatenate(pieces, axis=0)
                turned = turned + dot(kt_ref[row + off], dscore, ((1,), (0,)))
            own_ref[row] = turned.T * gq

        def key_line(row):
            pairs = qd_ref[pl.ds(row, SPAN)].reshape(SPAN * 2 * area, 2 * depth)
            grads = dot(w_ref[row + REACH], pairs, ((1,), (0,)))
            terms = grads[:, :depth] * gk + grads[:, depth:] * gv
            term_ref[0, row] = terms[:area]
            own_ref[row] = own_ref[row] + terms[area : 2 * area]
            term_ref[1, row] = terms[2 * area :]

        def collect(row):
            both(lambda side: t_copy(row, 1 - side).wait_recv())
            dnormed = own_ref[row]
            dnormed = dnormed + jnp.where(has_right, from_ref[0, row], 0.0)
            dnormed = dnormed + jnp.where(has_left, from_ref[1, row], 0.0)
            scaled = dnormed * gn
            own_ref[row] = scaled
            product = (x3_ref[1, row].astype(F32) * scaled).T
            part_ref[row // GROUP, pl.ds(row % GROUP, 1), :] = jnp.sum(
                product, axis=0, keepdims=True
            )

        def own_part(group):
            return pltpu.make_async_copy(
                part_ref.at[group], mean_ref.at[group, me], m_local.at[group]
            )

        def share(row):
            @pl.when(row % GROUP == GROUP - 1)
            def _():
                group = row // GROUP
                own_part(group).start()
                loop(1, HEADS, lambda hop: m_copy(group, me, to(hop)).start())

        def close(row):
            @pl.when(row % GROUP == GROUP - 1)
            def _():
                group = row // GROUP
                own_part(group).wait()
                loop(1, HEADS, lambda hop: m_copy(group, back(hop), me).wait_recv())
                means = jnp.sum(mean_ref[group], axis=0) / (rows * depth)
                for line in range(GROUP):
                    each = group * GROUP + line
                    inverse = jnp.broadcast_to(r3_ref[1, each], (area, area))
                    pull = (inverse * inverse * inverse * means[line : line + 1]).T
                    grad = (
                        cot_ref[each].astype(F32)
                        + inverse.T * own_ref[each]
                        - x3_ref[1, each].astype(F32) * pull
                    )
                    grad_ref[each] = grad.astype(BF16)

        def give_back(row):
            @pl.when(row % GROUP == GROUP - 1)
            def _():
                for line in range(GROUP):
                    g_copy(me, row - line).start()

        def send_terms(row):
            both(lambda side: t_copy(row, side).start())

        def pair(turn):
            first = 2 * turn

            @pl.when(jnp.logical_and(turn >= 3, first < rows))
            def _():
                key_line(first - 5)
                key_line(first - 4)
                score(first - 1, 1)
                grade(first, 0)
                score(first, 0)
                grade(first + 1, 1)

            @pl.when(turn < 3)
            def _():
                @pl.when(turn == 2)
                def _():
                    key_line(first - 4)

                @pl.when(turn > 0)
                def _():
                    score(first - 1, 1)

                grade(first, 0)
                score(first, 0)
                grade(first + 1, 1)

            @pl.when(first == rows)
            def _():
                key_line(first - 5)
                key_line(first - 4)
                score(first - 1, 1)

            @pl.when(first == rows + 2)
            def _():
                for line in (-5, -4, -3):
                    key_line(first + line)

            for part in range(2):
                for act, lag in (
                    (send_terms, 6),
                    (collect, 6 + TERMS_LAG),
                    (share, 7 + TERMS_LAG),
                    (close, 7 + TERMS_LAG + MEAN_LAG),
                    (give_back, 8 + TERMS_LAG + MEAN_LAG),
                ):
                    row = first + part - lag

                    @pl.when(jnp.logical_and(row >= 0, row < rows))
                    def _():
                        act(row)

        loop(0, (rows + 8 + TERMS_LAG + MEAN_LAG + 1) // 2, pair)

    @pl.when(pipe < pipes - 1)
    def _():
        loop(0, rows, lambda row: greet({"pipe": pipe + 1, "row": row}))

    @pl.when(pipe == pipes - 1)
    def _():
        out_ref[...] = jnp.zeros_like(out_ref)

    @pl.when(pipe > 0)
    def _():
        work()

    @pl.when(pipe < pipes - 1)
    def _():
        def wait_grad(row):
            remote(
                grad_ref.at[0], out_ref.at[:, head_lanes(row)], g_send.at[0], g_recv.at[row],
                {"pipe": pipe + 1, "row": row},
            ).wait_recv()

        loop(0, rows, wait_grad)

    @pl.when(pipe > 0)
    def _():
        def drain(hop):
            x_copy(me, to(hop)).wait_send()
            r_copy(me, to(hop)).wait_send()
            c_copy(me, to(hop)).wait_send()

        loop(1, HEADS, drain)

        def drain_row(row):
            both(lambda side: fx_copy(row, side).wait_send())
            both(lambda side: fr_copy(row, side).wait_send())
            both(lambda side: t_copy(row, side).wait_send())
            g_copy(me, row).wait_send()

        loop(0, rows, drain_row)

        def drain_group(group):
            loop(1, HEADS, lambda hop: m_copy(group, me, to(hop)).wait_send())

        loop(0, rows // GROUP, drain_group)


def per_device(saved_in, cotangent, section_gains):
    _, tall, across, width = saved_in.shape
    area = tall * across
    rows = HEADS
    wide = 3 * area
    x = saved_in.reshape(area, width)
    cot = cotangent.reshape(area, width)
    gains = section_gains.transpose(1, 0, 2)
    far = pl.BlockSpec(memory_space=pl.ANY)
    vmem = pl.BlockSpec(memory_space=pltpu.VMEM)
    dma = pltpu.SemaphoreType.DMA
    grad = pl.pallas_call(
        section_kernel,
        out_shape=jax.ShapeDtypeStruct((area, width), BF16),
        in_specs=[vmem, far, far, far],
        out_specs=vmem,
        scratch_shapes=[
            pltpu.VMEM((3, rows, area, HEAD_DIM), BF16),
            pltpu.VMEM((3, rows, 1, area), F32),
            pltpu.VMEM((rows, area, HEAD_DIM), BF16),
            pltpu.VMEM((gains.shape[0], 1, HEAD_DIM), F32),
            pltpu.VMEM((1, area), F32),
            pltpu.VMEM((2, wide, area), F32),
            pltpu.VMEM((rows + 4, wide, 2 * HEAD_DIM), BF16),
            pltpu.VMEM((rows + 4, HEAD_DIM, wide), BF16),
            pltpu.VMEM((rows + 4, 2 * area, 2 * HEAD_DIM), BF16),
            pltpu.VMEM((rows + 4, wide, SPAN * 2 * area), BF16),
            pltpu.VMEM((rows, SPAN, wide, area), F32),
            pltpu.VMEM((rows, 3 * SPAN, area), F32),
            pltpu.VMEM((rows, 1, area), F32),
            pltpu.VMEM((2, SPAN, wide, area), F32),
            pltpu.VMEM((rows, area, HEAD_DIM), F32),
            pltpu.VMEM((2, rows, area, HEAD_DIM), F32),
            pltpu.VMEM((2, rows, area, HEAD_DIM), F32),
            pltpu.VMEM((rows // GROUP, GROUP, area), F32),
            pltpu.VMEM((rows // GROUP, HEADS, GROUP, area), F32),
            pltpu.VMEM((rows, area, HEAD_DIM), BF16),
            dma((4,)),
            dma((HEADS,)), dma((HEADS,)), dma((HEADS,)), dma((HEADS,)), dma((HEADS,)), dma((HEADS,)),
            dma((2, HEADS)), dma((2, HEADS)), dma((2, HEADS)), dma((2, HEADS)),
            dma((2, rows)), dma((2, rows)),
            dma((rows // GROUP,)), dma((rows // GROUP, HEADS)), dma((rows // GROUP, HEADS)),
            dma((rows,)), dma((HEADS,)),
        ],
        compiler_params=pltpu.CompilerParams(
            collective_id=0, has_side_effects=True, vmem_limit_bytes=60 * 1024 * 1024
        ),
        name="section_backward",
    )(x, x, cot, gains)
    return grad.reshape(1, tall, across, width)


def solution(mesh):
    return jax.shard_map(
        per_device,
        mesh=mesh,
        in_specs=(
            P("pipe", "row", "col", None),
            P("pipe", "row", "col", None),
            P("pipe", None, None),
        ),
        out_specs=P("pipe", "row", "col", None),
        check_vma=False,
    )
```
